32 devices in a mesh: fsdp: 8 (over z, y), dp: 4 (over x, core).
Axes of the slice: x: 2, y: 2, z: 4, core: 2. Of those that a mesh axis runs over, the one named last changes fastest.
Arguments:
- tokens: bfloat16 [32, 1024, 768], P(('fsdp', 'dp')), may hold values from -6 to 6
- segment_ids: int32 [32, 1024], P(('fsdp', 'dp')), may hold values from 0 to 20, never falling along the last dimension, each value on 1 to 49 neighbouring positions
- cotangent: bfloat16 [32, 1024, 768], P(('fsdp', 'dp')), may hold values from -6 to 6
- ln1_gain: bfloat16 [768], P('fsdp'), may hold values from 0.25 to 1.75
- ln1_bias: bfloat16 [768], P('fsdp'), may hold values from -1.75 to 1.75
- qkv_weight: bfloat16 [768, 2304], P('fsdp'), may hold values from -0.21875 to 0.21875
- query_bias: bfloat16 [768], P('fsdp'), may hold values from -1.75 to 1.75
- value_bias: bfloat16 [768], P('fsdp'), may hold values from -1.75 to 1.75
- proj_weight: bfloat16 [768, 768], P('fsdp'), may hold values from -0.875 to 0.875
- proj_bias: bfloat16 [768], P('fsdp'), may hold values from -1.75 to 1.75
- ln2_gain: bfloat16 [768], P('fsdp'), may hold values from 0.25 to 1.75
- ln2_bias: bfloat16 [768], P('fsdp'), may hold values from -1.75 to 1.75
- fc1_weight: bfloat16 [768, 3072], P('fsdp'), may hold values from -0.21875 to 0.21875
- fc1_bias: bfloat16 [3072], P('fsdp'), may hold values from -1.75 to 1.75
- fc2_weight: bfloat16 [3072, 768], P('fsdp'), may hold values from -0.15625 to 0.15625
- fc2_bias: bfloat16 [768], P('fsdp'), may hold values from -1.75 to 1.75
Outputs:
- layer_out: bfloat16 [32, 1024, 768], P(('fsdp', 'dp'))
- input_grad: float32 [32, 1024, 768], P(('fsdp', 'dp'))
- grad_ln1_gain: float32 [768], P('fsdp')
- grad_ln1_bias: float32 [768], P('fsdp')
- grad_qkv_weight: float32 [768, 2304], P('fsdp')
- grad_query_bias: float32 [768], P('fsdp')
- grad_value_bias: float32 [768], P('fsdp')
- grad_proj_weight: float32 [768, 768], P('fsdp')
- grad_proj_bias: float32 [768], P('fsdp')
- grad_ln2_gain: float32 [768], P('fsdp')
- grad_ln2_bias: float32 [768], P('fsdp')
- grad_fc1_weight: float32 [768, 3072], P('fsdp')
- grad_fc1_bias: float32 [3072], P('fsdp')
- grad_fc2_weight: float32 [3072, 768], P('fsdp')
- grad_fc2_bias: float32 [768], P('fsdp')
The draws below stay inside these ranges and needn't reach their ends.
Inputs may be any that keep to these rules, and one draw needn't show every extreme that they name: `segment_ids`: within a row the ids never fall and each id covers 1 to 49 consecutive positions.
All inputs are finite; a program needn't handle non-finite values.
Results may differ from the reference program's by a relative error of at most 0.015.
Values may be sent and summed in bfloat16 or wider, within the bound.
No kernel may reach another device: no remote copies, remote signals or barrier semaphores. Data moves between devices by JAX's collectives and lax.ppermute only.
A program may use at most 256 MiB of HBM per device.

```python
import math
import jax
import jax.numpy as jnp
import numpy as np
from jax import lax

D = 768
HEADS = 12
HD = 64
FF = 3072
SEQ = 1024
SEG_MAX = 49
SEGS = 21
ROWS = 32


def with_spikes(values, rng, source, target, blocks, factor):
    owner, partner = [(jnp.arange(values.shape[axis_at]) // (values.shape[axis_at] // blocks)).reshape([-1 if axis == axis_at else 1 for axis in range(values.ndim)]) for axis_at in (source, target)]
    chosen = jax.random.permutation(rng, blocks)[partner]
    strong = (owner == chosen) | (owner == (partner + blocks // 2) % blocks)
    return jnp.where(strong, factor * values, values)


def steps_of(own_key, shape, shards, smallest, top_value):
    def one(position, blocks):
        draws = jax.random.uniform(jax.random.fold_in(jax.random.fold_in(own_key, 6), position), (blocks,), jnp.float32, smallest / len(shards), top_value / len(shards))
        return jnp.repeat(jnp.exp(draws), shape[position] // blocks).reshape((-1,) + (1,) * (len(shape) - position - 1))

    level = one(*shards[0])
    for cut in shards[1:]:
        level = level * one(*cut)
    return level


def profile(amount, total, reach, skew):
    portions = [(1 << 20) // math.isqrt(standing ** skew) + 1 for standing in range(2, amount + 1)]
    surplus, given = total - reach - (amount - 1), [1] * (amount - 1)
    while surplus > 0:
        free = [i for i in range(amount - 1) if given[i] < reach]
        whole, remaining = sum([portions[i] for i in free]), surplus
        for i in free:
            more = min(reach - given[i], max(1, remaining * portions[i] // whole), surplus)
            given[i] = given[i] + more
            surplus = surplus - more
    return np.array([reach] + given)


def ragged(key, number_of, total, bound, lean):
    if number_of == 2:
        one = jax.random.randint(key, (), max(1, total - bound), min(bound, total - 1) + 1)
        return jnp.stack([one, total - one])
    sizes = jnp.asarray(profile(number_of, total, bound, lean), jnp.int32)
    twos = (number_of - 1) // 2
    donor, sink = sizes[1:1 + 2 * twos:2], sizes[2:2 + 2 * twos:2]
    slack = jnp.minimum(donor - 1, bound - sink)
    moved = jax.random.randint(jax.random.fold_in(key, 1), (twos,), 0, 1 << 20) % (slack + 1)
    sizes = sizes.at[1:1 + 2 * twos:2].set(donor - moved).at[2:2 + 2 * twos:2].set(sink + moved)
    return sizes[jax.random.permutation(jax.random.fold_in(key, 2), number_of)]


def noise(rng, extent, deviation, most, cuts=(), held_as=jnp.bfloat16):
    values = deviation * jax.random.normal(rng, extent, jnp.float32)
    if cuts:
        values = values * steps_of(rng, extent, cuts, -0.22, 0.18)
    return jnp.clip(values, -most, most).astype(held_as)


def heavy_noise(rng, dims, spread, reach, shards, heavy, dtype=jnp.bfloat16):
    values = spread * jax.random.normal(rng, dims, jnp.float32)
    if shards:
        values = values * steps_of(rng, dims, shards, -0.22, 0.18)
    return jnp.clip(with_spikes(values, jax.random.fold_in(rng, 3), *heavy), -reach, reach).astype(dtype)


def setup_inputs(seed: int = 0) -> dict:
    key_of = jax.random.split(jax.random.key(seed), 17)
    return {
        "tokens": noise(key_of[0], (ROWS, SEQ, D), 1.0, 6.0, ((0, 32),)),
        "segment_ids": jax.vmap(lambda own: jnp.searchsorted(jnp.cumsum(ragged(own, SEGS, SEQ, SEG_MAX, 0)), jnp.arange(SEQ), side="right"))(jax.random.split(key_of[1], ROWS)).reshape((ROWS, SEQ)).astype(jnp.int32),
        "cotangent": heavy_noise(key_of[2], (ROWS, SEQ, D), 1.0, 6.0, ((0, 32),), (0, 2, 32, 2.75)),
        "ln1_gain": jnp.clip(1.0 + 0.15 * jax.random.normal(key_of[3], (D,), jnp.float32), 0.25, 1.75).astype(jnp.bfloat16),
        "ln1_bias": noise(key_of[4], (D,), 0.3, 1.75, ((0, 8),)),
        "qkv_weight": noise(key_of[5], (D, 3 * D), D ** -0.5, 0.21875, ((0, 8),)),
        "query_bias": noise(key_of[6], (D,), 0.3, 1.75, ((0, 8),)),
        "value_bias": noise(key_of[7], (D,), 0.3, 1.75, ((0, 8),)),
        "proj_weight": noise(key_of[8], (D, D), (D // 16) ** -0.5, 0.875, ((0, 8),)),
        "proj_bias": noise(key_of[9], (D,), 0.3, 1.75, ((0, 8),)),
        "ln2_gain": jnp.clip(1.0 + 0.15 * jax.random.normal(key_of[10], (D,), jnp.float32), 0.25, 1.75).astype(jnp.bfloat16),
        "ln2_bias": noise(key_of[11], (D,), 0.3, 1.75, ((0, 8),)),
        "fc1_weight": noise(key_of[12], (D, FF), D ** -0.5, 0.21875, ((0, 8),)),
        "fc1_bias": noise(key_of[13], (FF,), 0.3, 1.75, ((0, 8),)),
        "fc2_weight": noise(key_of[14], (FF, D), (FF // 2) ** -0.5, 0.15625, ((0, 8),)),
        "fc2_bias": noise(key_of[15], (D,), 0.3, 1.75, ((0, 8),)),
    }


@jax.custom_vjp
def low(v):
    return lax.optimization_barrier(v.astype(jnp.bfloat16)).astype(jnp.float32)

@jax.custom_vjp
def low_back(v):
    return v

def low_keep(v):
    return (low(v), None)

def low_pass(kept, grad):
    return (grad,)

def back_keep(v):
    return (v, None)

def back_low(kept, grad):
    return (low(grad),)
low.defvjp(low_keep, low_pass)
low_back.defvjp(back_keep, back_low)
epsilon = 1e-06
masked_fill = -1e+30

def dot_high(left, right):
    return jnp.dot(left, right, precision=lax.Precision.HIGHEST, preferred_element_type=jnp.float32)

def layer_norm(values, gain, shift):
    row_mean = lax.optimization_barrier(jnp.mean(values, axis=-1, keepdims=True))
    centred = values - row_mean
    variance = lax.optimization_barrier(jnp.mean(centred * centred, axis=-1, keepdims=True))
    return centred * lax.rsqrt(variance + epsilon) * gain + shift

def forward_row(row_tokens, row_segments, params):
    ln1_gain, ln1_bias, qkv_weight, query_bias, value_bias, proj_weight, proj_bias, ln2_gain, ln2_bias, fc1_weight, fc1_bias, fc2_weight, fc2_bias = params
    seq_len, width = row_tokens.shape
    normed_one = low(layer_norm(row_tokens, ln1_gain, ln1_bias))
    qkv_shift = jnp.concatenate([query_bias, jnp.zeros_like(query_bias), value_bias])
    qkv_all = low(low_back(dot_high(normed_one, qkv_weight) + qkv_shift))
    qkv_heads = qkv_all.reshape(seq_len, 3, HEADS, HD)
    query_part = qkv_heads[:, 0]
    key_part = qkv_heads[:, 1]
    value_part = qkv_heads[:, 2]
    scores = jnp.einsum('qhd,khd->hqk', query_part, key_part, precision=lax.Precision.HIGHEST) * HD ** (-0.5)
    scores = low_back(scores)
    same = row_segments[:, None] == row_segments[None, :]
    masked = jnp.where(same[None], scores, masked_fill)
    row_max = lax.optimization_barrier(jnp.max(masked, axis=-1, keepdims=True))
    expo = jnp.exp(masked - row_max)
    probs = low(expo / lax.optimization_barrier(jnp.sum(expo, axis=-1, keepdims=True)))
    context = jnp.einsum('hqk,khd->qhd', probs, value_part, precision=lax.Precision.HIGHEST).reshape(seq_len, width)
    context = low(low_back(context))
    attended = low_back(dot_high(context, proj_weight) + proj_bias)
    middle = row_tokens + attended
    normed_two = low(layer_norm(middle, ln2_gain, ln2_bias))
    hidden = low_back(dot_high(normed_two, fc1_weight) + fc1_bias)
    activated = low(jax.nn.gelu(hidden, approximate=False))
    branch = low_back(dot_high(activated, fc2_weight) + fc2_bias)
    return middle + branch

def reference(tokens, segment_ids, cotangent, ln1_gain, ln1_bias, qkv_weight, query_bias, value_bias, proj_weight, proj_bias, ln2_gain, ln2_bias, fc1_weight, fc1_bias, fc2_weight, fc2_bias):
    params = tuple((item.astype(jnp.float32) for item in (ln1_gain, ln1_bias, qkv_weight, query_bias, value_bias, proj_weight, proj_bias, ln2_gain, ln2_bias, fc1_weight, fc1_bias, fc2_weight, fc2_bias)))

    def one_row(totals, items):
        row_tokens, row_segments, row_cotangent = items

        def local_forward(token_values, param_values):
            return forward_row(token_values, row_segments, param_values)
        result, pullback = jax.vjp(local_forward, row_tokens.astype(jnp.float32), params)
        token_grad, param_grad = pullback(row_cotangent.astype(jnp.float32))
        totals = jax.tree.map(lambda first, second: first + second, totals, param_grad)
        return (totals, (result.astype(jnp.bfloat16), token_grad))
    zeros = tuple((jnp.zeros_like(item) for item in params))
    totals, (layer_out, input_grad) = lax.scan(one_row, zeros, (tokens, segment_ids, cotangent))
    return (layer_out, input_grad, totals[0], totals[1], totals[2], totals[3], totals[4], totals[5], totals[6], totals[7], totals[8], totals[9], totals[10], totals[11], totals[12])
```

```python
import jax
import jax.numpy as jnp
from jax import lax
from jax.sharding import PartitionSpec as P
from jax.experimental import pallas as pl
from jax.experimental.pallas import tpu as pltpu

HEADS = 12
HD = 64
SEG_MAX = 49
masked_fill = -1e30
PAIR = 2 * HD
QB = 128
WIN = 256


def dotf(a, b, ca, cb):
    return lax.dot_general(a, b, (((ca,), (cb,)), ((), ())), preferred_element_type=jnp.float32)


def window_start(i, seq):
    return min(max(i * QB - (WIN - QB) // 2, 0), seq - WIN)


def stack_heads(v):
    lane = lax.broadcasted_iota(jnp.int32, v.shape, 1)
    zero = jnp.zeros_like(v)
    return jnp.concatenate([jnp.where(lane < HD, v, zero), jnp.where(lane < HD, zero, v)], axis=0)


def fill_bias(seg_row, seg_col, bias_s, seq):
    for i in range(seq // QB):
        s = window_start(i, seq)
        same = seg_col[s : s + WIN, :] == seg_row[:, i * QB : (i + 1) * QB]
        bias_s[i] = jnp.where(same, 0.0, masked_fill)


def pick_heads(t):
    return jnp.concatenate([t[:HD, :QB], t[HD:, QB:]], axis=0)


def attend_kernel(seg_row, seg_col, q_ref, k_ref, v_ref, ctx_ref, lse_ref, bias_s):
    seq = q_ref.shape[0]

    @pl.when(pl.program_id(0) == 0)
    def _():
        fill_bias(seg_row, seg_col, bias_s, seq)

    for i in range(seq // QB):
        s = window_start(i, seq)
        rows = slice(i * QB, (i + 1) * QB)
        keys = k_ref[s : s + WIN, :]
        values = v_ref[s : s + WIN, :]
        q_st = stack_heads(q_ref[rows, :] * jnp.bfloat16(HD**-0.5))
        st = dotf(keys, q_st, 1, 1)
        bias = bias_s[i]
        st = jnp.concatenate([st[:, :QB] + bias, st[:, QB:] + bias], axis=1)
        top = jnp.max(st, axis=0, keepdims=True)
        p = jnp.exp(st - top)
        total = jnp.sum(p, axis=0, keepdims=True)
        ctx_t = dotf(values, p.astype(jnp.bfloat16), 0, 0) * (1.0 / total)
        ctx_ref[rows, :] = jnp.transpose(pick_heads(ctx_t)).astype(jnp.bfloat16)
        lse = top + jnp.log(total)
        lse_ref[0, 0:1, rows] = lse[:, :QB]
        lse_ref[0, 1:2, rows] = lse[:, QB:]


def attend_back_kernel(
    seg_row, seg_col, q_ref, k_ref, v_ref, dctx_ref, lse_ref, dqkv_ref, colsum_ref, bias_s, dk_s, dv_s
):
    seq = q_ref.shape[0]

    @pl.when(pl.program_id(0) == 0)
    def _():
        fill_bias(seg_row, seg_col, bias_s, seq)

    dk_s[...] = jnp.zeros_like(dk_s)
    dv_s[...] = jnp.zeros_like(dv_s)
    for i in range(seq // QB):
        s = window_start(i, seq)
        rows = slice(i * QB, (i + 1) * QB)
        win = slice(s, s + WIN)
        keys = k_ref[win, :]
        values = v_ref[win, :]
        q_st = stack_heads(q_ref[rows, :] * jnp.bfloat16(HD**-0.5))
        d_st = stack_heads(dctx_ref[rows, :])
        st = dotf(keys, q_st, 1, 1)
        bias = bias_s[i]
        lse_a = lse_ref[0, 0:1, rows]
        lse_b = lse_ref[0, 1:2, rows]
        st = jnp.concatenate([st[:, :QB] + bias - lse_a, st[:, QB:] + bias - lse_b], axis=1)
        p = jnp.exp(st)
        dp = dotf(values, d_st, 1, 1)
        ds = (p * (dp - jnp.sum(dp * p, axis=0, keepdims=True))).astype(jnp.bfloat16)
        dv_s[win, :] += dotf(p.astype(jnp.bfloat16), d_st, 1, 0)
        dk_s[win, :] += dotf(ds, q_st, 1, 0)
        dq_t = pick_heads(dotf(keys, ds, 0, 0)) * (HD**-0.5)
        dqkv_ref[0, rows, :] = jnp.transpose(dq_t).astype(jnp.bfloat16)
    dqkv_ref[1] = dk_s[...].astype(jnp.bfloat16)
    dqkv_ref[2] = dv_s[...].astype(jnp.bfloat16)
    for g in range(3):
        colsum_ref[g] = jnp.sum(dqkv_ref[g].astype(jnp.float32), axis=0, keepdims=True)


def attention(qkv, seg):
    seq = qkv.shape[0]
    pairs = HEADS // 2
    full = lambda *shape: pl.BlockSpec(shape, lambda h: (0,) * len(shape))
    col = lambda g: pl.BlockSpec((seq, PAIR), lambda h, g=g: (0, g * pairs + h))
    return pl.pallas_call(
        attend_kernel,
        grid=(pairs,),
        in_specs=[full(1, seq), full(seq, 1), col(0), col(1), col(2)],
        out_specs=[
            pl.BlockSpec((seq, PAIR), lambda h: (0, h)),
            pl.BlockSpec((1, 2, seq), lambda h: (h, 0, 0)),
        ],
        out_shape=[
            jax.ShapeDtypeStruct((seq, HEADS * HD), jnp.bfloat16),
            jax.ShapeDtypeStruct((pairs, 2, seq), jnp.float32),
        ],
        scratch_shapes=[pltpu.VMEM((seq // QB, WIN, QB), jnp.float32)],
        name="attend",
    )(seg.reshape(1, seq), seg.reshape(seq, 1), qkv, qkv, qkv)


def attention_back(qkv, seg, dctx, lse):
    seq = qkv.shape[0]
    pairs = HEADS // 2
    full = lambda *shape: pl.BlockSpec(shape, lambda h: (0,) * len(shape))
    col = lambda g: pl.BlockSpec((seq, PAIR), lambda h, g=g: (0, g * pairs + h))
    return pl.pallas_call(
        attend_back_kernel,
        grid=(pairs,),
        in_specs=[
            full(1, seq),
            full(seq, 1),
            col(0),
            col(1),
            col(2),
            pl.BlockSpec((seq, PAIR), lambda h: (0, h)),
            pl.BlockSpec((1, 2, seq), lambda h: (h, 0, 0)),
        ],
        out_specs=[
            pl.BlockSpec((3, seq, PAIR), lambda h: (0, 0, h)),
            pl.BlockSpec((3, 1, PAIR), lambda h: (0, 0, h)),
        ],
        out_shape=[
            jax.ShapeDtypeStruct((3, seq, HEADS * HD), jnp.bfloat16),
            jax.ShapeDtypeStruct((3, 1, HEADS * HD), jnp.float32),
        ],
        scratch_shapes=[
            pltpu.VMEM((seq // QB, WIN, QB), jnp.float32),
            pltpu.VMEM((seq, PAIR), jnp.float32),
            pltpu.VMEM((seq, PAIR), jnp.float32),
        ],
        name="attend_back",
    )(seg.reshape(1, seq), seg.reshape(seq, 1), qkv, qkv, qkv, dctx, lse)


epsilon = 1e-06
RING_MAX = 16


def ring_order(n):
    if n % 2:
        return list(range(n))
    return list(range(0, n, 2)) + list(range(n - 1, 0, -2))


def core_pairs(dp):
    return [(d, d ^ 1) for d in range(dp)]


def core_swap(v, dp):
    return lax.ppermute(v, "dp", core_pairs(dp))


def ring_gather(piece, n, dp):
    order = ring_order(n)
    place = {f: p for p, f in enumerate(order)}
    up = [(order[p], order[(p + 1) % n]) for p in range(n)]
    down = [(order[(p + 1) % n], order[p]) for p in range(n)]
    here = jnp.asarray([place[f] for f in range(n)], jnp.int32)[lax.axis_index("fsdp")]
    source = lambda shift: jnp.asarray(order, jnp.int32)[(here + shift) % n]
    pieces = [(piece, source(0))]
    right = left = piece
    for s in range(1, (n - 1) // 2 + 1):
        right = lax.ppermute(right, "fsdp", up)
        left = lax.ppermute(left, "fsdp", down)
        pieces += [(right, source(n - s)), (left, source(s))]
    if n % 2 == 0:
        half = n // 2
        if n > 2:
            last = jnp.where(lax.axis_index("dp") % 2 == 0, right, left)
        else:
            last = piece
        both = []
        for d in range(dp):
            both += [(a * dp + d, b * dp + d) for a, b in (up if d % 2 == 0 else down)]
        pieces.append((lax.ppermute(last, ("fsdp", "dp"), both), source(half)))
    return pieces


def assemble(pieces, others, table, moves, out_shapes):
    count = len(pieces)

    def kernel(table_ref, *refs):
        ins, rest = refs[: 2 * count], refs[2 * count :]
        outs, sems = rest[:-1], rest[-1]
        core = table_ref[count]
        copies = []
        for k in range(2 * count):
            where = table_ref[k % count]
            c = core if k < count else 1 - core
            for o, r0, rows, c0, cols, step, core_step, first, col in moves:
                if core_step == 0 and k >= count:
                    continue
                row = pl.multiple_of(where * step + c * core_step + first, 8)
                copy = pltpu.make_async_copy(
                    ins[k].at[pl.ds(r0, rows), pl.ds(c0, cols)],
                    outs[o].at[pl.ds(row, rows), pl.ds(col, cols)],
                    sems.at[len(copies)],
                )
                copy.start()
                copies.append(copy)
        for copy in copies:
            copy.wait()

    total = 2 * count * len(moves)
    any_space = pl.BlockSpec(memory_space=pl.ANY)
    return pl.pallas_call(
        kernel,
        grid_spec=pltpu.PrefetchScalarGridSpec(
            num_scalar_prefetch=1,
            grid=(),
            in_specs=[any_space] * (2 * count),
            out_specs=[any_space] * len(out_shapes),
            scratch_shapes=[pltpu.SemaphoreType.DMA((total,))],
        ),
        out_shape=[jax.ShapeDtypeStruct(s, jnp.bfloat16) for s in out_shapes],
        name="assemble",
    )(table, *pieces, *others)


def gather_group(piece, n, dp, moves, out_shapes):
    got = ring_gather(piece, n, dp)
    pieces = [p for p, _ in got]
    others = [core_swap(p, dp) for p in pieces]
    table = jnp.stack([f for _, f in got] + [lax.axis_index("dp") % 2]).astype(jnp.int32)
    return assemble(pieces, others, table, moves, out_shapes)


def take(v, i, axis):
    return lax.dynamic_index_in_dim(v, i, axis, keepdims=False)


def wide(v):
    return v.astype(jnp.float32)


def low(v):
    return v.astype(jnp.bfloat16)


def reduce_group(blocks, n, dp):
    _, rows, columns = blocks.shape
    half = columns // 2
    f = lax.axis_index("fsdp")
    d = lax.axis_index("dp")
    core = d % 2
    slab = lambda c: lax.dynamic_slice_in_dim(blocks, c * half, half, 2)
    both = wide(slab(core)) + wide(core_swap(slab(1 - core), dp))
    pair = both.reshape(n // 2, 2, rows, half)
    flip = [(i, i ^ 1) for i in range(n)]
    sent = lax.ppermute(low(take(pair, 1 - f % 2, 1)), "fsdp", flip)
    mine = take(pair, f % 2, 1) + wide(sent)
    z = f // 2
    total = take(mine, z, 0)
    for k in range(1, n // 2):
        hop = [(i, ((i // 2) ^ k) * 2 + i % 2) for i in range(n)]
        total = total + wide(lax.ppermute(low(take(mine, z ^ k, 0)), "fsdp", hop))
    total = low(total)
    if dp > 2:
        total = low(wide(total) + wide(lax.ppermute(total, "dp", [(i, i ^ 2) for i in range(dp)])))
    other = core_swap(total, dp)
    first = core == 0
    return jnp.concatenate([jnp.where(first, total, other), jnp.where(first, other, total)], axis=1)


def gelu_kernel(x_ref, w_ref, b_ref, act_ref, slope_ref):
    rows = 256
    for r in range(x_ref.shape[0] // rows):
        at = slice(r * rows, (r + 1) * rows)
        h = jnp.dot(x_ref[at, :], w_ref[...], preferred_element_type=jnp.float32) + b_ref[...]
        size = jnp.abs(h)
        t = 1.0 / (1.0 + (0.3275911 * 0.7071067811865476) * size)
        e = jnp.exp(-0.5 * h * h)
        poly = t * (
            0.5 * 0.254829592
            + t * (-0.5 * 0.284496736 + t * (0.5 * 1.421413741 + t * (-0.5 * 1.453152027 + t * (0.5 * 1.061405429))))
        )
        tail = poly * e
        upper = jnp.where(h >= 0.0, 1.0 - tail, tail)
        act_ref[at, :] = (h * upper).astype(jnp.bfloat16)
        slope_ref[at, :] = (upper + (h * 0.3989422804014327) * e).astype(jnp.bfloat16)


def gelu_layer(x, w, b):
    rows, width = x.shape
    ff = w.shape[1]
    tile = 512
    out = pl.BlockSpec((rows, tile), lambda j: (0, j))
    return pl.pallas_call(
        gelu_kernel,
        grid=(ff // tile,),
        in_specs=[
            pl.BlockSpec((rows, width), lambda j: (0, 0)),
            pl.BlockSpec((width, tile), lambda j: (0, j)),
            pl.BlockSpec((1, tile), lambda j: (0, j)),
        ],
        out_specs=[out, out],
        out_shape=[jax.ShapeDtypeStruct((rows, ff), jnp.bfloat16)] * 2,
        name="gelu_layer",
    )(x, w, b.reshape(1, ff))


def norm_parts(v):
    c = v - jnp.mean(v, axis=-1, keepdims=True)
    r = lax.rsqrt(jnp.mean(c * c, axis=-1, keepdims=True) + epsilon)
    return c * r, r


def norm_back(dn, x, r, gain):
    u = dn * gain
    e = r * (u - jnp.mean(u, axis=-1, keepdims=True) - x * jnp.mean(u * x, axis=-1, keepdims=True))
    return e, jnp.sum(dn * x, axis=0), jnp.sum(dn, axis=0)


def column_sum(v):
    return jnp.sum(v.astype(jnp.float32), axis=0)


def matmul(a, b, ca, cb):
    return lax.dot_general(a, b, (((ca,), (cb,)), ((), ())), preferred_element_type=jnp.float32)


def gather_all(shards, n, dp):
    qkv, proj, fc1, fc2, vectors = shards
    rows, wide_columns = qkv.shape
    width = proj.shape[1]
    ff = fc1.shape[1]
    if n > RING_MAX or dp != 4:
        gather = lambda v: lax.all_gather(v, "fsdp", axis=0, tiled=True)
        small = lax.all_gather(vectors, "fsdp", axis=0)
        return gather(qkv), gather(proj), gather(fc1), gather(fc2), small
    core = lax.axis_index("dp") % 2
    cut = lambda v: lax.dynamic_slice_in_dim(v, core * (v.shape[0] // 2), v.shape[0] // 2, 0)
    half = rows // 2
    top = jnp.concatenate([cut(qkv), cut(proj)], axis=1)
    extra = jnp.pad(vectors.reshape(1, -1), ((0, 7), (0, top.shape[1] - vectors.shape[0])))
    first = jnp.concatenate([top, extra], axis=0)
    wqkv, wproj, small = gather_group(
        first,
        n,
        dp,
        [
            (0, 0, half, 0, wide_columns, rows, half, 0, 0),
            (1, 0, half, wide_columns, width, rows, half, 0, 0),
            (2, half, 8, 0, top.shape[1], 8, 0, 0, 0),
        ],
        [(n * rows, wide_columns), (n * rows, width), (n * 8, top.shape[1])],
    )
    small = small.reshape(n, 8, -1)[:, 0, : vectors.shape[0]]
    parts = ff // width
    deep = cut(fc2).reshape(parts, half, width)
    second = jnp.concatenate([cut(fc1)] + [jnp.concatenate([deep[j] for j in range(parts)], axis=1)], axis=0)
    second, _ = lax.optimization_barrier((second, wproj))
    w1, w2 = gather_group(
        second,
        n,
        dp,
        [(0, 0, half, 0, ff, rows, half, 0, 0)]
        + [
            (1, half, half, j * width, width, rows * parts, half * parts, j * half, 0)
            for j in range(parts)
        ],
        [(n * rows, ff), (n * rows * parts, width)],
    )
    return wqkv, wproj, w1, w2, small


def reduce_all(blocks, n, dp):
    if n > RING_MAX or dp != 4:
        flat = blocks.reshape(n * blocks.shape[1], blocks.shape[2])
        return low(lax.psum(lax.psum_scatter(flat, "fsdp", scatter_dimension=0, tiled=True), "dp"))
    return reduce_group(blocks, n, dp)


def per_device(n, dp, tokens, segment_ids, cotangent, *params):
    (
        ln1_gain,
        ln1_bias,
        qkv_weight,
        query_bias,
        value_bias,
        proj_weight,
        proj_bias,
        ln2_gain,
        ln2_bias,
        fc1_weight,
        fc1_bias,
        fc2_weight,
        fc2_bias,
    ) = params
    _, seq, width = tokens.shape
    shard = ln1_gain.shape[0]
    ff = fc1_weight.shape[1]
    vectors = jnp.concatenate(
        [ln1_gain, ln1_bias, query_bias, value_bias, proj_bias, ln2_gain, ln2_bias, fc2_bias, fc1_bias]
    )
    wqkv, wproj, w1, w2, small = gather_all((qkv_weight, proj_weight, fc1_weight, fc2_weight, vectors), n, dp)
    small = wide(small)
    whole = [small[:, j * shard : (j + 1) * shard].reshape(-1) for j in range(8)]
    g1, b1, bq, bv, bp, g2, b2, b_fc2 = whole
    b_fc1 = small[:, 8 * shard :].reshape(-1)

    flat = wide(tokens.reshape(seq, width))
    seg = segment_ids.reshape(seq)
    x1, r1 = norm_parts(flat)
    n1 = low(x1 * g1 + b1)
    shift = jnp.concatenate([bq, jnp.zeros_like(bq), bv])
    qkv = low(matmul(n1, wqkv, 1, 0) + shift)
    ctx, lse = attention(qkv, seg)
    middle = flat + (matmul(ctx, wproj, 1, 0) + bp)
    x2, r2 = norm_parts(middle)
    n2 = low(x2 * g2 + b2)
    act, slope = gelu_layer(n2, w1, b_fc1)
    layer_out = low(middle + (matmul(act, w2, 1, 0) + b_fc2))

    d_branch = cotangent.reshape(seq, width)
    upstream = wide(d_branch)
    grad_fc2_bias = column_sum(d_branch)
    grad_fc2 = low(matmul(act, d_branch, 0, 0))
    out_fc2 = reduce_all(grad_fc2.reshape(n, ff // n, width), n, dp)
    d_hidden = low(matmul(d_branch, w2, 1, 1) * wide(slope))
    grad_fc1_bias = column_sum(d_hidden)
    grad_fc1 = low(matmul(n2, d_hidden, 0, 0))
    out_fc1 = reduce_all(grad_fc1.reshape(n, shard, ff), n, dp)
    d_norm_two = matmul(d_hidden, w1, 1, 1)
    e2, grad_ln2_gain, grad_ln2_bias = norm_back(d_norm_two, x2, r2, g2)
    d_middle = upstream + e2
    d_attn = low(d_middle)
    grad_proj_bias = column_sum(d_attn)
    grad_proj = low(matmul(ctx, d_attn, 0, 0))
    d_ctx = low(matmul(d_attn, wproj, 1, 1))
    d_qkv, sums = attention_back(qkv, seg, d_ctx, lse)
    grads = [low(matmul(n1, d_qkv[g], 0, 0)) for g in range(3)]
    d_norm_one = sum(matmul(d_qkv[g], wqkv[:, g * width : (g + 1) * width], 1, 1) for g in range(3))
    e1, grad_ln1_gain, grad_ln1_bias = norm_back(d_norm_one, x1, r1, g1)
    input_grad = d_middle + e1

    top = jnp.concatenate(grads + [grad_proj], axis=1).reshape(n, shard, 4 * width)
    tiny = jnp.stack(
        [
            grad_ln1_gain,
            grad_ln1_bias,
            sums[0, 0],
            sums[2, 0],
            grad_proj_bias,
            grad_ln2_gain,
            grad_ln2_bias,
            grad_fc2_bias,
        ]
    ).reshape(8, n, shard)
    tiny = jnp.concatenate([tiny.transpose(1, 0, 2).reshape(n, -1), grad_fc1_bias.reshape(n, -1)], axis=1)
    tiny = jnp.pad(low(tiny)[:, None, :], ((0, 0), (0, 7), (0, 4 * width - tiny.shape[1])))
    out_last = reduce_all(jnp.concatenate([top, tiny], axis=1), n, dp)
    out_last = wide(out_last)
    line = out_last[shard]
    vec = [line[j * shard : (j + 1) * shard] for j in range(8)]
    return (
        layer_out.reshape(tokens.shape),
        input_grad.reshape(tokens.shape),
        vec[0],
        vec[1],
        out_last[:shard, : 3 * width],
        vec[2],
        vec[3],
        out_last[:shard, 3 * width :],
        vec[4],
        vec[5],
        vec[6],
        wide(out_fc1),
        line[8 * shard : 8 * shard + ff // n],
        wide(out_fc2),
        vec[7],
    )


def solution(mesh):
    n, dp = mesh.shape["fsdp"], mesh.shape["dp"]
    rows = P(("fsdp", "dp"), None, None)
    vec, mat = P("fsdp"), P("fsdp", None)
    params = (vec, vec, mat, vec, vec, mat, vec, vec, vec, mat, vec, mat, vec)
    return jax.shard_map(
        lambda *args: per_device(n, dp, *args),
        mesh=mesh,
        in_specs=(rows, P(("fsdp", "dp"), None), rows) + params,
        out_specs=(rows, rows) + params,
        check_vma=False,
    )
```

```python
import jax
import jax.numpy as jnp
from jax import lax
from jax.sharding import PartitionSpec as P
from jax.experimental import pallas as pl
from jax.experimental.pallas import tpu as pltpu

HEADS = 12
HD = 64
SEG_MAX = 49
masked_fill = -1e30
PAIR = 2 * HD
QB = 128
WIN = 256


def dotf(a, b, ca, cb):
    return lax.dot_general(a, b, (((ca,), (cb,)), ((), ())), preferred_element_type=jnp.float32)


def window_start(i, seq):
    return min(max(i * QB - (WIN - QB) // 2, 0), seq - WIN)


def stack_heads(v):
    lane = lax.broadcasted_iota(jnp.int32, v.shape, 1)
    zero = jnp.zeros_like(v)
    return jnp.concatenate([jnp.where(lane < HD, v, zero), jnp.where(lane < HD, zero, v)], axis=0)


def fill_bias(seg_row, seg_col, bias_s, seq):
    for i in range(seq // QB):
        s = window_start(i, seq)
        same = seg_col[s : s + WIN, :] == seg_row[:, i * QB : (i + 1) * QB]
        bias_s[i] = jnp.where(same, 0.0, masked_fill)


def pick_heads(t):
    return jnp.concatenate([t[:HD, :QB], t[HD:, QB:]], axis=0)


def attend_kernel(seg_row, seg_col, qkv_ref, *refs):
    ctx_ref, lse_ref, bias_s = refs[-3:]
    seq = qkv_ref.shape[0]

    @pl.when(pl.program_id(0) == 0)
    def _():
        fill_bias(seg_row, seg_col, bias_s, seq)

    for i in range(seq // QB):
        s = window_start(i, seq)
        rows = slice(i * QB, (i + 1) * QB)
        keys = qkv_ref[s : s + WIN, PAIR : 2 * PAIR]
        values = qkv_ref[s : s + WIN, 2 * PAIR :]
        q_st = stack_heads(qkv_ref[rows, :PAIR] * jnp.bfloat16(HD**-0.5))
        st = dotf(keys, q_st, 1, 1)
        bias = bias_s[i]
        st = jnp.concatenate([st[:, :QB] + bias, st[:, QB:] + bias], axis=1)
        top = jnp.max(st, axis=0, keepdims=True)
        p = jnp.exp(st - top)
        total = jnp.sum(p, axis=0, keepdims=True)
        ctx_t = dotf(values, p.astype(jnp.bfloat16), 0, 0) * (1.0 / total)
        ctx_ref[rows, :] = jnp.transpose(pick_heads(ctx_t)).astype(jnp.bfloat16)
        lse = top + jnp.log(total)
        lse_ref[0, 0:1, rows] = lse[:, :QB]
        lse_ref[0, 1:2, rows] = lse[:, QB:]


def attend_back_kernel(seg_row, seg_col, qkv_ref, dctx_ref, lse_ref, *refs):
    dqkv_ref, colsum_ref, bias_s, dk_s, dv_s = refs[-5:]
    seq = qkv_ref.shape[0]

    @pl.when(pl.program_id(0) == 0)
    def _():
        fill_bias(seg_row, seg_col, bias_s, seq)

    dk_s[...] = jnp.zeros_like(dk_s)
    dv_s[...] = jnp.zeros_like(dv_s)
    for i in range(seq // QB):
        s = window_start(i, seq)
        rows = slice(i * QB, (i + 1) * QB)
        win = slice(s, s + WIN)
        keys = qkv_ref[win, PAIR : 2 * PAIR]
        values = qkv_ref[win, 2 * PAIR :]
        q_st = stack_heads(qkv_ref[rows, :PAIR] * jnp.bfloat16(HD**-0.5))
        d_st = stack_heads(dctx_ref[rows, :])
        st = dotf(keys, q_st, 1, 1)
        bias = bias_s[i]
        lse_a = lse_ref[0, 0:1, rows]
        lse_b = lse_ref[0, 1:2, rows]
        st = jnp.concatenate([st[:, :QB] + bias - lse_a, st[:, QB:] + bias - lse_b], axis=1)
        p = jnp.exp(st)
        dp = dotf(values, d_st, 1, 1)
        ds = (p * (dp - jnp.sum(dp * p, axis=0, keepdims=True))).astype(jnp.bfloat16)
        dv_s[win, :] += dotf(p.astype(jnp.bfloat16), d_st, 1, 0)
        dk_s[win, :] += dotf(ds, q_st, 1, 0)
        dq_t = pick_heads(dotf(keys, ds, 0, 0)) * (HD**-0.5)
        dqkv_ref[rows, :PAIR] = jnp.transpose(dq_t).astype(jnp.bfloat16)
    dqkv_ref[:, PAIR : 2 * PAIR] = dk_s[...].astype(jnp.bfloat16)
    dqkv_ref[:, 2 * PAIR :] = dv_s[...].astype(jnp.bfloat16)
    colsum_ref[...] = jnp.sum(dqkv_ref[...].astype(jnp.float32), axis=0, keepdims=True)


ANY = pl.BlockSpec(memory_space=pl.ANY)
PARTS = 2
GROUP = HEADS // 2 // PARTS


def attention(qkv, seg, part, before=()):
    seq = qkv.shape[0]
    off = part * GROUP
    full = lambda *shape: pl.BlockSpec(shape, lambda h: (0,) * len(shape))
    return pl.pallas_call(
        attend_kernel,
        grid=(GROUP,),
        in_specs=[full(1, seq), full(seq, 1), pl.BlockSpec((seq, 3 * PAIR), lambda h: (0, off + h))]
        + [ANY] * len(before),
        out_specs=[
            pl.BlockSpec((seq, PAIR), lambda h: (0, off + h)),
            pl.BlockSpec((1, 2, seq), lambda h: (off + h, 0, 0)),
        ],
        out_shape=[
            jax.ShapeDtypeStruct((seq, HEADS * HD), jnp.bfloat16),
            jax.ShapeDtypeStruct((HEADS // 2, 2, seq), jnp.float32),
        ],
        scratch_shapes=[pltpu.VMEM((seq // QB, WIN, QB), jnp.float32)],
        input_output_aliases={3 + i: i for i in range(len(before))},
        name=f"attend_{part}",
    )(seg.reshape(1, seq), seg.reshape(seq, 1), qkv, *before)


def attention_back(qkv, seg, dctx, lse, part, before=()):
    seq = qkv.shape[0]
    off = part * GROUP
    full = lambda *shape: pl.BlockSpec(shape, lambda h: (0,) * len(shape))
    return pl.pallas_call(
        attend_back_kernel,
        grid=(GROUP,),
        in_specs=[
            full(1, seq),
            full(seq, 1),
            pl.BlockSpec((seq, 3 * PAIR), lambda h: (0, off + h)),
            pl.BlockSpec((seq, PAIR), lambda h: (0, off + h)),
            pl.BlockSpec((1, 2, seq), lambda h: (off + h, 0, 0)),
        ]
        + [ANY] * len(before),
        out_specs=[
            pl.BlockSpec((seq, 3 * PAIR), lambda h: (0, off + h)),
            pl.BlockSpec((1, 3 * PAIR), lambda h: (0, off + h)),
        ],
        out_shape=[
            jax.ShapeDtypeStruct((seq, 3 * HEADS * HD), jnp.bfloat16),
            jax.ShapeDtypeStruct((1, 3 * HEADS * HD), jnp.float32),
        ],
        scratch_shapes=[
            pltpu.VMEM((seq // QB, WIN, QB), jnp.float32),
            pltpu.VMEM((seq, PAIR), jnp.float32),
            pltpu.VMEM((seq, PAIR), jnp.float32),
        ],
        input_output_aliases={5 + i: i for i in range(len(before))},
        name=f"attend_back_{part}",
    )(seg.reshape(1, seq), seg.reshape(seq, 1), qkv, dctx, lse, *before)


epsilon = 1e-06
RING_MAX = 16


def wide(v):
    return v.astype(jnp.float32)


def low(v):
    return v.astype(jnp.bfloat16)


def tie(*vs):
    return lax.optimization_barrier(vs)


def ring_order(n):
    return list(range(0, n, 2)) + list(range(n - 1, 0, -2))


class Ring:
    def __init__(self, n, dp):
        self.n, self.dp, self.steps = n, dp, n // 2 - 1
        order = ring_order(n)
        place = {f: p for p, f in enumerate(order)}
        at = lambda p: order[p % n]
        self.pairs = []
        for p in range(n):
            for d in range(dp):
                s = 1 if d % 2 == 0 else -1
                self.pairs.append((at(p) * dp + d, at(p + s) * dp + d))
        rows = []
        for f in range(n):
            for c in range(2):
                s, p = 1 - 2 * c, place[f]
                back = [at(p - s * k) for k in range(1, self.steps + 1)]
                ahead = [at(p + s * k) for k in range(1, self.steps + 1)]
                rows.append([f] + back + ahead + [at(p + n // 2), c])
        index = lax.axis_index("fsdp") * 2 + lax.axis_index("dp") % 2
        self.table = lax.dynamic_index_in_dim(jnp.asarray(rows, jnp.int32), index, 0, keepdims=False)
        self.core = self.table[-1]
        self.opposite = self.table[-2]

    def ahead(self, k):
        return self.table[self.steps + k] if k else self.table[0]

    def send(self, v):
        return lax.ppermute(v, ("fsdp", "dp"), self.pairs)

    def core_swap(self, v):
        return lax.ppermute(v, "dp", [(d, d ^ 1) for d in range(self.dp)])

    def chip_swap(self, v):
        return lax.ppermute(v, "dp", [(d, d ^ 2) for d in range(self.dp)])

    def half(self, v, rows):
        return lax.dynamic_slice_in_dim(v, self.core * (rows // 2), rows // 2, 0)

    def sum_all(self, v):
        v = v + self.core_swap(v)
        v = v + self.chip_swap(v)
        step = 1
        while step < self.n:
            v = v + lax.ppermute(v, "fsdp", [(i, i ^ step) for i in range(self.n)])
            step *= 2
        return v


def place_pieces(table_ref, pieces, write):
    count = len(pieces) - 2
    core = table_ref[count + 1]
    for k in range(count):
        for h in range(2):
            write(table_ref[k], h, pieces[k], h)
    write(table_ref[count], core, pieces[count], 0)
    write(table_ref[count], 1 - core, pieces[count + 1], 0)


def natural_columns(width):
    return [((h * 3 + g) * PAIR, g * width + h * PAIR) for h in range(width // PAIR) for g in range(3)]


def assemble_first(table, pieces, n, rows, width, shard):
    half = rows // 2
    cols = 4 * width

    def kernel(table_ref, *refs):
        ins, (wqkv_ref, wproj_ref, vec_ref, b1_ref, small) = refs[:-5], refs[-5:]

        def write(f, h, ref, first):
            at = slice(first * half, (first + 1) * half)
            for dst, src in natural_columns(width):
                wqkv_ref[f, h, :, dst : dst + PAIR] = ref[at, src : src + PAIR]
            wproj_ref[f, h] = ref[at, 3 * width :]

        place_pieces(table_ref, ins, write)
        count = len(ins) - 2
        for k in range(count):
            small[table_ref[k]] = wide(ins[k][rows : rows + 8, : 2 * PAIR])
        small[table_ref[count]] = wide(ins[count][half : half + 8, : 2 * PAIR])
        vec_ref[...] = jnp.concatenate([small[f][:, :shard] for f in range(n)], axis=1)
        b1_ref[...] = jnp.concatenate(
            [small[f][r : r + 1, PAIR : PAIR + shard] for f in range(n) for r in range(4)], axis=1
        )

    vm = lambda: pl.BlockSpec(memory_space=pltpu.VMEM)
    wqkv, wproj, vec, b1 = pl.pallas_call(
        kernel,
        grid_spec=pltpu.PrefetchScalarGridSpec(
            num_scalar_prefetch=1,
            grid=(),
            in_specs=[vm() for _ in pieces],
            out_specs=[vm() for _ in range(4)],
            scratch_shapes=[pltpu.VMEM((n, 8, 2 * PAIR), jnp.float32)],
        ),
        out_shape=[
            jax.ShapeDtypeStruct((n, 2, half, 3 * width), jnp.bfloat16),
            jax.ShapeDtypeStruct((n, 2, half, width), jnp.bfloat16),
            jax.ShapeDtypeStruct((8, width), jnp.float32),
            jax.ShapeDtypeStruct((1, 4 * n * shard), jnp.float32),
        ],
        name="assemble_first",
    )(table, *pieces)
    return wqkv.reshape(n * rows, 3 * width), wproj.reshape(n * rows, width), vec, b1


def assemble(table, pieces, n):
    rows, cols = pieces[0].shape
    half = rows // 2
    tile = min(cols, 384)

    def kernel(table_ref, *refs):
        ins, out_ref = refs[:-1], refs[-1]

        def write(f, h, ref, first):
            out_ref[f, h] = ref[first * half : (first + 1) * half, :]

        place_pieces(table_ref, ins, write)

    out = pl.pallas_call(
        kernel,
        grid_spec=pltpu.PrefetchScalarGridSpec(
            num_scalar_prefetch=1,
            grid=(cols // tile,),
            in_specs=[pl.BlockSpec((p.shape[0], tile), lambda j, t: (0, j)) for p in pieces],
            out_specs=pl.BlockSpec((n, 2, half, tile), lambda j, t: (0, 0, 0, j)),
        ),
        out_shape=jax.ShapeDtypeStruct((n, 2, half, cols), jnp.bfloat16),
        name="assemble",
    )(table, *pieces)
    return out.reshape(n * rows, cols)


def pick(index, grads):
    count = index.shape[0]
    rows = grads[0].shape[1]
    cols = [g.shape[2] for g in grads]

    def kernel(index_ref, *refs):
        out_ref, first = refs[-1], 0
        for ref, c in zip(refs, cols):
            out_ref[:, :, first : first + c] = ref[...]
            first += c

    return pl.pallas_call(
        kernel,
        grid_spec=pltpu.PrefetchScalarGridSpec(
            num_scalar_prefetch=1,
            grid=(count,),
            in_specs=[pl.BlockSpec((1, rows, c), lambda k, t: (t[k], 0, 0)) for c in cols],
            out_specs=pl.BlockSpec((1, rows, sum(cols)), lambda k, t: (k, 0, 0)),
        ),
        out_shape=jax.ShapeDtypeStruct((count, rows, sum(cols)), jnp.bfloat16),
        name="pick",
    )(index, *grads)


class Reduction:
    def __init__(self, ring, grads):
        self.ring = ring
        rows = grads[0].shape[0] // ring.n
        self.rows = rows
        self.grads = [g.reshape(2 * ring.n, rows // 2, g.shape[1]) for g in grads]
        t, m = ring.table, ring.steps
        back = t[1 : m + 1]
        whole = (2 * back[:, None] + jnp.arange(2, dtype=jnp.int32)[None, :]).reshape(-1)
        index = jnp.concatenate([whole, (2 * ring.opposite + 1 - ring.core).reshape(1)])
        self.outgoing = pick(index, self.grads)

    def own(self, first, count):
        parts = [wide(lax.dynamic_slice_in_dim(g, first, count, 0)) for g in self.grads]
        return parts[0] if len(parts) == 1 else jnp.concatenate(parts, axis=2)

    def cores(self):
        self.other = self.ring.core_swap(self.outgoing)

    def step(self, k):
        ring, m = self.ring, self.ring.steps
        if k == 0:
            v = self.own(2 * ring.opposite + ring.core, 1) + wide(self.other[2 * m :])
        else:
            d = m + 1 - k
            v = self.own(2 * ring.ahead(d), 2) + wide(self.other[2 * d - 2 : 2 * d])
            if k == 1:
                at = lax.broadcasted_iota(jnp.int32, v.shape, 0)
                v = v + jnp.where(at == ring.core, wide(self.got), 0.0)
            else:
                v = v + wide(self.got)
        self.got = ring.send(low(v))

    def join(self):
        self.part = low(self.own(2 * self.ring.table[0], 2) + wide(self.got))
        self.part_other = self.ring.core_swap(self.part)

    def chips(self):
        self.both = low(wide(self.part) + wide(self.part_other))
        self.both_other = self.ring.chip_swap(self.both)

    def result(self):
        v = wide(self.both) + wide(self.both_other)
        return v.reshape(self.rows, v.shape[2])


def gelu_kernel(x_ref, w_ref, b_ref, act_ref, slope_ref):
    rows = 256
    for r in range(x_ref.shape[0] // rows):
        at = slice(r * rows, (r + 1) * rows)
        h = jnp.dot(x_ref[at, :], w_ref[...], preferred_element_type=jnp.float32) + b_ref[...]
        size = jnp.abs(h)
        t = 1.0 / (1.0 + (0.3275911 * 0.7071067811865476) * size)
        e = jnp.exp(-0.5 * h * h)
        poly = t * (
            0.5 * 0.254829592
            + t * (-0.5 * 0.284496736 + t * (0.5 * 1.421413741 + t * (-0.5 * 1.453152027 + t * (0.5 * 1.061405429))))
        )
        tail = poly * e
        upper = jnp.where(h >= 0.0, 1.0 - tail, tail)
        act_ref[at, :] = (h * upper).astype(jnp.bfloat16)
        slope_ref[at, :] = (upper + (h * 0.3989422804014327) * e).astype(jnp.bfloat16)


TILE = 512


def gelu_layer(x, w, b):
    rows, width = x.shape
    ff = w.shape[1]
    out = pl.BlockSpec((rows, TILE), lambda j: (0, j))
    return pl.pallas_call(
        gelu_kernel,
        grid=(ff // TILE,),
        in_specs=[
            pl.BlockSpec((rows, width), lambda j: (0, 0)),
            pl.BlockSpec((width, TILE), lambda j: (0, j)),
            pl.BlockSpec((1, TILE), lambda j: (0, j)),
        ],
        out_specs=[out, out],
        out_shape=[jax.ShapeDtypeStruct((rows, ff), jnp.bfloat16)] * 2,
        name="gelu_layer",
    )(x, w, b)


def gelu_ring(x, table, pieces, b, n, part, before=()):
    rows, width = x.shape
    shard, ff = pieces[0].shape
    half = shard // 2
    steps = ff // TILE // PARTS
    off = part * steps

    def kernel(table_ref, x_ref, b_ref, *refs):
        ins = refs[: len(pieces)]
        act_ref, slope_ref, w_ref, scratch = refs[-4:]

        def write(f, h, ref, first):
            v = ref[first * half : (first + 1) * half, :]
            scratch[f, h] = v
            w_ref[f, h] = v

        place_pieces(table_ref, ins, write)
        gelu_kernel(x_ref, scratch_view(scratch), b_ref, act_ref, slope_ref)

    class scratch_view:
        def __init__(self, ref):
            self.ref = ref

        def __getitem__(self, _):
            return self.ref[...].reshape(width, TILE)

    out = pl.BlockSpec((rows, TILE), lambda j, t: (0, off + j))
    first = 3 + len(pieces)
    act, slope, w = pl.pallas_call(
        kernel,
        grid_spec=pltpu.PrefetchScalarGridSpec(
            num_scalar_prefetch=1,
            grid=(steps,),
            in_specs=[
                pl.BlockSpec((rows, width), lambda j, t: (0, 0)),
                pl.BlockSpec((1, TILE), lambda j, t: (0, off + j)),
            ]
            + [pl.BlockSpec((p.shape[0], TILE), lambda j, t: (0, off + j)) for p in pieces]
            + [ANY] * len(before),
            out_specs=[out, out, pl.BlockSpec((n, 2, half, TILE), lambda j, t: (0, 0, 0, off + j))],
            scratch_shapes=[pltpu.VMEM((n, 2, half, TILE), jnp.bfloat16)],
        ),
        out_shape=[jax.ShapeDtypeStruct((rows, ff), jnp.bfloat16)] * 2
        + [jax.ShapeDtypeStruct((n, 2, half, ff), jnp.bfloat16)],
        input_output_aliases={first + i: i for i in range(len(before))},
        name=f"gelu_ring_{part}",
    )(table, x, b, *pieces, *before)
    return act, slope, w


def norm_parts(v):
    c = v - jnp.mean(v, axis=-1, keepdims=True)
    r = lax.rsqrt(jnp.mean(c * c, axis=-1, keepdims=True) + epsilon)
    return c * r, r


def column_sum(v):
    return jnp.sum(v.astype(jnp.float32), axis=0, keepdims=True)


def norm_back(dn, x, r, gain):
    u = dn * gain
    e = r * (u - jnp.mean(u, axis=-1, keepdims=True) - x * jnp.mean(u * x, axis=-1, keepdims=True))
    return e, column_sum(dn * x), column_sum(dn)


def matmul(a, b, ca, cb):
    return lax.dot_general(a, b, (((ca,), (cb,)), ((), ())), preferred_element_type=jnp.float32)


def pair_order(v, width):
    return v.reshape(v.shape[0], 3, width // PAIR, PAIR).transpose(0, 2, 1, 3).reshape(v.shape[0], 3 * width)


def natural_order(v, width):
    return jnp.concatenate(
        [v[:, (h * 3 + g) * PAIR : (h * 3 + g + 1) * PAIR] for g in range(3) for h in range(width // PAIR)], axis=1
    )


def qkv_shift(vec):
    rows = [vec[2:3], jnp.zeros_like(vec[2:3]), vec[3:4]]
    return pair_order(jnp.concatenate(rows, axis=1), vec.shape[1])


def pack_small(rows, b1, n):
    width = rows[0].shape[1]
    shard = width // n

    def kernel(*refs):
        out_ref = refs[-1]
        out_ref[...] = jnp.zeros_like(out_ref)
        every = jnp.concatenate([r[...] for r in refs[:8]], axis=0)
        line = refs[8][...]
        for f in range(n):
            out_ref[f, 0:8, 0:shard] = every[:, f * shard : (f + 1) * shard]
            for r in range(4):
                first = (4 * f + r) * shard
                out_ref[f, 8 + r : 9 + r, 0:shard] = line[:, first : first + shard]

    return pl.pallas_call(
        kernel, out_shape=jax.ShapeDtypeStruct((n, 16, PAIR), jnp.float32), name="pack_small"
    )(*rows, b1)


def layer_ring(n, dp, tokens, segment_ids, cotangent, params):
    (ln1_gain, ln1_bias, qkv_weight, query_bias, value_bias, proj_weight, proj_bias) = params[:7]
    (ln2_gain, ln2_bias, fc1_weight, fc1_bias, fc2_weight, fc2_bias) = params[7:]
    _, seq, width = tokens.shape
    shard = ln1_gain.shape[0]
    ff = fc1_weight.shape[1]
    ring = Ring(n, dp)
    table = ring.table
    swap = ring.core_swap

    eight = jnp.stack([ln1_gain, ln1_bias, query_bias, value_bias, proj_bias, ln2_gain, ln2_bias, fc2_bias])
    four = fc1_bias.reshape(4, shard)
    small = jnp.concatenate(
        [jnp.pad(eight, ((0, 0), (0, PAIR - shard))), jnp.pad(four, ((0, 4), (0, 4 * width - PAIR - shard)))], axis=1
    )
    top = jnp.concatenate([jnp.concatenate([qkv_weight, proj_weight], axis=1), small], axis=0)
    a = [top]
    for _ in range(ring.steps):
        a.append(ring.send(a[-1]))
    a_last = ring.send(jnp.concatenate([ring.half(a[-1][:shard], shard), a[-1][shard:]], axis=0))
    pieces = a + [swap(v) for v in a[1:]] + [a_last, swap(a_last)]
    wqkv, wproj, vec, b_fc1 = assemble_first(table, pieces, n, shard, width, shard)
    g1, b1, bp, g2, b2, b_fc2 = (vec[j : j + 1] for j in (0, 1, 4, 5, 6, 7))

    c0, _ = tie(fc1_weight, a_last)
    c1 = ring.send(c0)
    flat = wide(tokens.reshape(seq, width))
    seg = segment_ids.reshape(seq)
    x1, r1 = norm_parts(flat)
    n1 = low(x1 * g1 + b1)
    qkv = low(matmul(n1, wqkv, 1, 0) + qkv_shift(vec))
    qkv, c1 = tie(qkv, c1)
    c2, d1 = ring.send(c1), swap(c1)
    ctx, lse = attention(qkv, seg, 0)
    ctx, lse, c2, d1 = tie(ctx, lse, c2, d1)
    c3, d2 = ring.send(c2), swap(c2)
    ctx, lse = attention(qkv, seg, 1, (ctx, lse))
    ctx, lse, c3, d2 = tie(ctx, lse, c3, d2)
    c4, d3 = ring.send(ring.half(c3, shard)), swap(c3)
    middle = wide(tokens.reshape(seq, width)) + (matmul(ctx, wproj, 1, 0) + bp)
    x2, r2 = norm_parts(middle)
    n2 = low(x2 * g2 + b2)
    n2, c4, d3 = tie(n2, c4, d3)
    d4 = swap(c4)
    pieces = [c0, c1, c2, c3, d1, d2, d3, c4, d4]
    e0, _ = tie(fc2_weight, c4)
    e1 = ring.send(e0)
    act, slope, w1 = gelu_ring(n2, table, pieces, b_fc1, n, 0)
    act, slope, w1, e1 = tie(act, slope, w1, e1)
    e2, f1 = ring.send(e1), swap(e1)
    act, slope, w1 = gelu_ring(n2, table, pieces, b_fc1, n, 1, (act, slope, w1))
    w1 = w1.reshape(width, ff)
    act, e2, f1 = tie(act, e2, f1)
    e3, f2 = ring.send(e2), swap(e2)
    d_branch = cotangent.reshape(seq, width)
    grad_fc2 = low(matmul(act, d_branch, 0, 0))
    grad_fc2, e3, f2 = tie(grad_fc2, e3, f2)
    e4, f3 = ring.send(ring.half(e3, ff // n)), swap(e3)
    two = Reduction(ring, [grad_fc2])
    two.outgoing, e4, f3 = tie(two.outgoing, e4, f3)
    f4 = swap(e4)
    two.cores()
    w2 = assemble(table, [e0, e1, e2, e3, f1, f2, f3, e4, f4], n)

    w2, two.other = tie(w2, two.other)
    two.step(0)
    d_hidden = low(matmul(d_branch, w2, 1, 1) * wide(slope))
    d_hidden, two.got = tie(d_hidden, two.got)
    two.step(1)
    grad_fc1 = low(matmul(n2, d_hidden, 0, 0))
    grad_fc1, two.got = tie(grad_fc1, two.got)
    two.step(2)
    d_norm_two = matmul(d_hidden, w1, 1, 1)
    e2_, grad_ln2_gain, grad_ln2_bias = norm_back(d_norm_two, x2, r2, g2)
    d_middle = wide(d_branch) + e2_
    d_attn = low(d_middle)
    d_attn, two.got = tie(d_attn, two.got)
    two.step(3)
    grad_proj = low(matmul(ctx, d_attn, 0, 0))
    one = Reduction(ring, [grad_fc1, grad_proj])
    d_ctx = low(matmul(d_attn, wproj, 1, 1))
    d_ctx, one.outgoing, two.got = tie(d_ctx, one.outgoing, two.got)
    one.cores()
    two.join()
    d_qkv, sums = attention_back(qkv, seg, d_ctx, lse, 0)
    d_qkv, sums, one.other, two.part_other = tie(d_qkv, sums, one.other, two.part_other)
    one.step(0)
    two.chips()
    d_qkv, sums = attention_back(qkv, seg, d_ctx, lse, 1, (d_qkv, sums))
    d_qkv, sums, one.got, two.both_other = tie(d_qkv, sums, one.got, two.both_other)
    one.step(1)
    out_fc2 = two.result()
    grad_qkv = low(matmul(n1, d_qkv, 0, 0))
    grad_qkv, one.got = tie(grad_qkv, one.got)
    one.step(2)
    last = Reduction(ring, [grad_qkv])
    last.outgoing, one.got = tie(last.outgoing, one.got)
    last.cores()
    one.step(3)
    d_norm_one = matmul(d_qkv, wqkv, 1, 1)
    e1_, grad_ln1_gain, grad_ln1_bias = norm_back(d_norm_one, x1, r1, g1)
    input_grad = d_middle + e1_
    input_grad, grad_ln1_gain, grad_ln1_bias, last.other, one.got = tie(
        input_grad, grad_ln1_gain, grad_ln1_bias, last.other, one.got
    )
    last.step(0)
    one.join()
    sums = natural_order(sums, width)
    tiny = pack_small(
        [
            grad_ln1_gain,
            grad_ln1_bias,
            sums[:, :width],
            sums[:, 2 * width :],
            column_sum(d_attn),
            grad_ln2_gain,
            grad_ln2_bias,
            column_sum(d_branch),
        ],
        column_sum(d_hidden),
        n,
    )
    tiny, last.got, one.part_other = tie(tiny, last.got, one.part_other)
    last.step(1)
    one.chips()
    layer_out = low(middle + (matmul(act, w2, 1, 0) + b_fc2))
    layer_out, last.got, one.both_other = tie(layer_out, last.got, one.both_other)
    last.step(2)
    tiny = ring.sum_all(tiny)
    out_one = one.result()
    last.step(3)
    last.join()
    last.chips()
    out_qkv = natural_order(last.result(), width)
    mine = lax.dynamic_index_in_dim(tiny, table[0], 0, keepdims=False)
    line = [mine[j, :shard] for j in range(8)]
    return (
        layer_out.reshape(tokens.shape),
        input_grad.reshape(tokens.shape),
        line[0],
        line[1],
        out_qkv,
        line[2],
        line[3],
        out_one[:, ff:],
        line[4],
        line[5],
        line[6],
        out_one[:, :ff],
        mine[8:12, :shard].reshape(4 * shard),
        out_fc2,
        line[7],
    )


def layer_plain(tokens, segment_ids, cotangent, params):
    gather = lambda v: lax.all_gather(v, "fsdp", axis=0, tiled=True)
    whole = [gather(v) for v in params]
    vec = wide(jnp.stack([whole[j] for j in (0, 1, 3, 4, 6, 7, 8, 12)]))
    _, seq, width = tokens.shape
    wqkv, wproj, w1, w2 = pair_order(whole[2], width), whole[5], whole[9], whole[11]
    b_fc1 = wide(whole[10]).reshape(1, -1)
    g1, b1, bp, g2, b2, b_fc2 = (vec[j : j + 1] for j in (0, 1, 4, 5, 6, 7))
    flat = wide(tokens.reshape(seq, width))
    seg = segment_ids.reshape(seq)
    x1, r1 = norm_parts(flat)
    n1 = low(x1 * g1 + b1)
    qkv = low(matmul(n1, wqkv, 1, 0) + qkv_shift(vec))
    kept = attention(qkv, seg, 0)
    ctx, lse = attention(qkv, seg, 1, kept)
    middle = flat + (matmul(ctx, wproj, 1, 0) + bp)
    x2, r2 = norm_parts(middle)
    n2 = low(x2 * g2 + b2)
    act, slope = gelu_layer(n2, w1, b_fc1)
    layer_out = low(middle + (matmul(act, w2, 1, 0) + b_fc2))
    d_branch = cotangent.reshape(seq, width)
    d_hidden = low(matmul(d_branch, w2, 1, 1) * wide(slope))
    e2, grad_ln2_gain, grad_ln2_bias = norm_back(matmul(d_hidden, w1, 1, 1), x2, r2, g2)
    d_middle = wide(d_branch) + e2
    d_attn = low(d_middle)
    d_ctx = low(matmul(d_attn, wproj, 1, 1))
    kept = attention_back(qkv, seg, d_ctx, lse, 0)
    d_qkv, sums = attention_back(qkv, seg, d_ctx, lse, 1, kept)
    sums = natural_order(sums, width)
    e1, grad_ln1_gain, grad_ln1_bias = norm_back(matmul(d_qkv, wqkv, 1, 1), x1, r1, g1)

    def reduce(v):
        return lax.psum(lax.psum_scatter(v, "fsdp", scatter_dimension=0, tiled=True), "dp")

    line = lambda v: reduce(v.reshape(-1))
    return (
        layer_out.reshape(tokens.shape),
        (d_middle + e1).reshape(tokens.shape),
        line(grad_ln1_gain),
        line(grad_ln1_bias),
        natural_order(reduce(matmul(n1, d_qkv, 0, 0)), width),
        line(sums[:, :width]),
        line(sums[:, 2 * width :]),
        reduce(matmul(ctx, d_attn, 0, 0)),
        line(column_sum(d_attn)),
        line(grad_ln2_gain),
        line(grad_ln2_bias),
        reduce(matmul(n2, d_hidden, 0, 0)),
        line(column_sum(d_hidden)),
        reduce(matmul(act, d_branch, 0, 0)),
        line(column_sum(d_branch)),
    )


def per_device(n, dp, tokens, segment_ids, cotangent, *params):
    small_ring = dp == 4 and 4 <= n <= RING_MAX and n & (n - 1) == 0
    if small_ring and params[0].shape[0] % 16 == 0:
        return layer_ring(n, dp, tokens, segment_ids, cotangent, params)
    return layer_plain(tokens, segment_ids, cotangent, params)


def solution(mesh):
    n, dp = mesh.shape["fsdp"], mesh.shape["dp"]
    rows = P(("fsdp", "dp"), None, None)
    vec, mat = P("fsdp"), P("fsdp", None)
    params = (vec, vec, mat, vec, vec, mat, vec, vec, vec, mat, vec, mat, vec)
    return jax.shard_map(
        lambda *args: per_device(n, dp, *args),
        mesh=mesh,
        in_specs=(rows, P(("fsdp", "dp"), None), rows) + params,
        out_specs=(rows, rows) + params,
        check_vma=False,
    )
```

```python
import jax
import jax.numpy as jnp
from jax import lax
from jax.sharding import PartitionSpec as P
from jax.experimental import pallas as pl
from jax.experimental.pallas import tpu as pltpu

HEADS = 12
HD = 64
SEG_MAX = 49
masked_fill = -1e30
PAIR = 2 * HD
QB = 128
WIN = 256


def dotf(a, b, ca, cb):
    return lax.dot_general(a, b, (((ca,), (cb,)), ((), ())), preferred_element_type=jnp.float32)


def window_start(i, seq):
    return min(max(i * QB - (WIN - QB) // 2, 0), seq - WIN)


def stack_heads(v):
    lane = lax.broadcasted_iota(jnp.int32, v.shape, 1)
    zero = jnp.zeros_like(v)
    return jnp.concatenate([jnp.where(lane < HD, v, zero), jnp.where(lane < HD, zero, v)], axis=0)


def fill_bias(seg_row, seg_col, bias_s, seq):
    for i in range(seq // QB):
        s = window_start(i, seq)
        same = seg_col[s : s + WIN, :] == seg_row[:, i * QB : (i + 1) * QB]
        bias_s[i] = jnp.where(same, 0.0, masked_fill)


def pick_heads(t):
    return jnp.concatenate([t[:HD, :QB], t[HD:, QB:]], axis=0)


def attend_kernel(seg_row, seg_col, qkv_ref, *refs):
    ctx_ref, lse_ref, bias_s = refs[-3:]
    seq = qkv_ref.shape[0]

    @pl.when(pl.program_id(0) == 0)
    def _():
        fill_bias(seg_row, seg_col, bias_s, seq)

    for i in range(seq // QB):
        s = window_start(i, seq)
        rows = slice(i * QB, (i + 1) * QB)
        keys = qkv_ref[s : s + WIN, PAIR : 2 * PAIR]
        values = qkv_ref[s : s + WIN, 2 * PAIR :]
        q_st = stack_heads(qkv_ref[rows, :PAIR] * jnp.bfloat16(HD**-0.5))
        st = dotf(keys, q_st, 1, 1)
        bias = bias_s[i]
        st = jnp.concatenate([st[:, :QB] + bias, st[:, QB:] + bias], axis=1)
        top = jnp.max(st, axis=0, keepdims=True)
        p = jnp.exp(st - top)
        total = jnp.sum(p, axis=0, keepdims=True)
        ctx_t = dotf(values, p.astype(jnp.bfloat16), 0, 0) * (1.0 / total)
        ctx_ref[rows, :] = jnp.transpose(pick_heads(ctx_t)).astype(jnp.bfloat16)
        lse = top + jnp.log(total)
        lse_ref[0, 0:1, rows] = lse[:, :QB]
        lse_ref[0, 1:2, rows] = lse[:, QB:]


def attend_back_kernel(seg_row, seg_col, qkv_ref, dctx_ref, lse_ref, *refs):
    dqkv_ref, colsum_ref, bias_s, dk_s, dv_s = refs[-5:]
    seq = qkv_ref.shape[0]

    @pl.when(pl.program_id(0) == 0)
    def _():
        fill_bias(seg_row, seg_col, bias_s, seq)

    dk_s[...] = jnp.zeros_like(dk_s)
    dv_s[...] = jnp.zeros_like(dv_s)
    for i in range(seq // QB):
        s = window_start(i, seq)
        rows = slice(i * QB, (i + 1) * QB)
        win = slice(s, s + WIN)
        keys = qkv_ref[win, PAIR : 2 * PAIR]
        values = qkv_ref[win, 2 * PAIR :]
        q_st = stack_heads(qkv_ref[rows, :PAIR] * jnp.bfloat16(HD**-0.5))
        d_st = stack_heads(dctx_ref[rows, :])
        st = dotf(keys, q_st, 1, 1)
        bias = bias_s[i]
        lse_a = lse_ref[0, 0:1, rows]
        lse_b = lse_ref[0, 1:2, rows]
        st = jnp.concatenate([st[:, :QB] + bias - lse_a, st[:, QB:] + bias - lse_b], axis=1)
        p = jnp.exp(st)
        dp = dotf(values, d_st, 1, 1)
        ds = (p * (dp - jnp.sum(dp * p, axis=0, keepdims=True))).astype(jnp.bfloat16)
        dv_s[win, :] += dotf(p.astype(jnp.bfloat16), d_st, 1, 0)
        dk_s[win, :] += dotf(ds, q_st, 1, 0)
        dq_t = pick_heads(dotf(keys, ds, 0, 0)) * (HD**-0.5)
        dqkv_ref[rows, :PAIR] = jnp.transpose(dq_t).astype(jnp.bfloat16)
    dqkv_ref[:, PAIR : 2 * PAIR] = dk_s[...].astype(jnp.bfloat16)
    dqkv_ref[:, 2 * PAIR :] = dv_s[...].astype(jnp.bfloat16)
    colsum_ref[...] = jnp.sum(dqkv_ref[...].astype(jnp.float32), axis=0, keepdims=True)


ANY = pl.BlockSpec(memory_space=pl.ANY)
PARTS = 2
GROUP = HEADS // 2 // PARTS


def attention(qkv, seg, part, before=()):
    seq = qkv.shape[0]
    off = part * GROUP
    full = lambda *shape: pl.BlockSpec(shape, lambda h: (0,) * len(shape))
    return pl.pallas_call(
        attend_kernel,
        grid=(GROUP,),
        in_specs=[full(1, seq), full(seq, 1), pl.BlockSpec((seq, 3 * PAIR), lambda h: (0, off + h))]
        + [ANY] * len(before),
        out_specs=[
            pl.BlockSpec((seq, PAIR), lambda h: (0, off + h)),
            pl.BlockSpec((1, 2, seq), lambda h: (off + h, 0, 0)),
        ],
        out_shape=[
            jax.ShapeDtypeStruct((seq, HEADS * HD), jnp.bfloat16),
            jax.ShapeDtypeStruct((HEADS // 2, 2, seq), jnp.float32),
        ],
        scratch_shapes=[pltpu.VMEM((seq // QB, WIN, QB), jnp.float32)],
        input_output_aliases={3 + i: i for i in range(len(before))},
        name=f"attend_{part}",
    )(seg.reshape(1, seq), seg.reshape(seq, 1), qkv, *before)


def attention_back(qkv, seg, dctx, lse, part, before=()):
    seq = qkv.shape[0]
    off = part * GROUP
    full = lambda *shape: pl.BlockSpec(shape, lambda h: (0,) * len(shape))
    return pl.pallas_call(
        attend_back_kernel,
        grid=(GROUP,),
        in_specs=[
            full(1, seq),
            full(seq, 1),
            pl.BlockSpec((seq, 3 * PAIR), lambda h: (0, off + h)),
            pl.BlockSpec((seq, PAIR), lambda h: (0, off + h)),
            pl.BlockSpec((1, 2, seq), lambda h: (off + h, 0, 0)),
        ]
        + [ANY] * len(before),
        out_specs=[
            pl.BlockSpec((seq, 3 * PAIR), lambda h: (0, off + h)),
            pl.BlockSpec((1, 3 * PAIR), lambda h: (0, off + h)),
        ],
        out_shape=[
            jax.ShapeDtypeStruct((seq, 3 * HEADS * HD), jnp.bfloat16),
            jax.ShapeDtypeStruct((1, 3 * HEADS * HD), jnp.float32),
        ],
        scratch_shapes=[
            pltpu.VMEM((seq // QB, WIN, QB), jnp.float32),
            pltpu.VMEM((seq, PAIR), jnp.float32),
            pltpu.VMEM((seq, PAIR), jnp.float32),
        ],
        input_output_aliases={5 + i: i for i in range(len(before))},
        name=f"attend_back_{part}",
    )(seg.reshape(1, seq), seg.reshape(seq, 1), qkv, dctx, lse, *before)


epsilon = 1e-06
RING_MAX = 16


def wide(v):
    return v.astype(jnp.float32)


def low(v):
    return v.astype(jnp.bfloat16)


def tie(*vs):
    return lax.optimization_barrier(vs)


def ring_order(n):
    return list(range(0, n, 2)) + list(range(n - 1, 0, -2))


class Ring:
    def __init__(self, n, dp):
        self.n, self.dp, self.steps = n, dp, n // 2 - 1
        order = ring_order(n)
        place = {f: p for p, f in enumerate(order)}
        at = lambda p: order[p % n]
        self.pairs = []
        for p in range(n):
            for d in range(dp):
                s = 1 if d % 2 == 0 else -1
                self.pairs.append((at(p) * dp + d, at(p + s) * dp + d))
        rows = []
        for f in range(n):
            for c in range(2):
                s, p = 1 - 2 * c, place[f]
                back = [at(p - s * k) for k in range(1, self.steps + 1)]
                ahead = [at(p + s * k) for k in range(1, self.steps + 1)]
                rows.append([f] + back + ahead + [at(p + n // 2), c])
        index = lax.axis_index("fsdp") * 2 + lax.axis_index("dp") % 2
        self.table = lax.dynamic_index_in_dim(jnp.asarray(rows, jnp.int32), index, 0, keepdims=False)
        self.core = self.table[-1]
        self.opposite = self.table[-2]
        self.index = reduce_index(self)

    def send(self, v):
        return lax.ppermute(v, ("fsdp", "dp"), self.pairs)

    def core_swap(self, v):
        return lax.ppermute(v, "dp", [(d, d ^ 1) for d in range(self.dp)])

    def chip_swap(self, v):
        return lax.ppermute(v, "dp", [(d, d ^ 2) for d in range(self.dp)])

    def half(self, v, rows):
        return lax.dynamic_slice_in_dim(v, self.core * (rows // 2), rows // 2, 0)


def place_pieces(table_ref, pieces, write):
    count = len(pieces) - 2
    core = table_ref[count + 1]
    for k in range(count):
        for h in range(2):
            write(table_ref[k], h, pieces[k], h)
    write(table_ref[count], core, pieces[count], 0)
    write(table_ref[count], 1 - core, pieces[count + 1], 0)


def natural_columns(width):
    return [((h * 3 + g) * PAIR, g * width + h * PAIR) for h in range(width // PAIR) for g in range(3)]


def assemble_first(table, pieces, n, rows, width, shard):
    half = rows // 2
    cols = 4 * width

    def kernel(table_ref, *refs):
        ins, (wqkv_ref, wproj_ref, vec_ref, b1_ref, small) = refs[:-5], refs[-5:]

        def write(f, h, ref, first):
            at = slice(first * half, (first + 1) * half)
            for dst, src in natural_columns(width):
                wqkv_ref[f, h, :, dst : dst + PAIR] = ref[at, src : src + PAIR]
            wproj_ref[f, h] = ref[at, 3 * width :]

        place_pieces(table_ref, ins, write)
        count = len(ins) - 2
        for k in range(count):
            small[table_ref[k]] = wide(ins[k][rows : rows + 8, : 2 * PAIR])
        small[table_ref[count]] = wide(ins[count][half : half + 8, : 2 * PAIR])
        vec_ref[...] = jnp.concatenate([small[f][:, :shard] for f in range(n)], axis=1)
        b1_ref[...] = jnp.concatenate(
            [small[f][r : r + 1, PAIR : PAIR + shard] for f in range(n) for r in range(4)], axis=1
        )

    vm = lambda: pl.BlockSpec(memory_space=pltpu.VMEM)
    wqkv, wproj, vec, b1 = pl.pallas_call(
        kernel,
        grid_spec=pltpu.PrefetchScalarGridSpec(
            num_scalar_prefetch=1,
            grid=(),
            in_specs=[vm() for _ in pieces],
            out_specs=[vm() for _ in range(4)],
            scratch_shapes=[pltpu.VMEM((n, 8, 2 * PAIR), jnp.float32)],
        ),
        out_shape=[
            jax.ShapeDtypeStruct((n, 2, half, 3 * width), jnp.bfloat16),
            jax.ShapeDtypeStruct((n, 2, half, width), jnp.bfloat16),
            jax.ShapeDtypeStruct((8, width), jnp.float32),
            jax.ShapeDtypeStruct((1, 4 * n * shard), jnp.float32),
        ],
        name="assemble_first",
    )(table, *pieces)
    return wqkv.reshape(n * rows, 3 * width), wproj.reshape(n * rows, width), vec, b1


def sort_blocks(index, split, grads):
    count = index.shape[0]
    rows = grads[0].shape[1]
    cols = [g.shape[2] for g in grads]

    def kernel(index_ref, *refs):
        ins, (a_ref, b_ref, sems) = refs[:-3], refs[-3:]
        copies = []
        for k in range(count):
            out, at = (a_ref, k) if k < split else (b_ref, k - split)
            first = 0
            for ref, c in zip(ins, cols):
                copy = pltpu.make_async_copy(
                    ref.at[index_ref[k]], out.at[at, :, pl.ds(first, c)], sems.at[len(copies)]
                )
                copy.start()
                copies.append(copy)
                first += c
        for copy in copies:
            copy.wait()

    vm = lambda: pl.BlockSpec(memory_space=pltpu.VMEM)
    return pl.pallas_call(
        kernel,
        grid_spec=pltpu.PrefetchScalarGridSpec(
            num_scalar_prefetch=1,
            grid=(),
            in_specs=[ANY] * len(grads),
            out_specs=[vm(), vm()],
            scratch_shapes=[pltpu.SemaphoreType.DMA((count * len(grads),))],
        ),
        out_shape=[
            jax.ShapeDtypeStruct((split, rows, sum(cols)), jnp.bfloat16),
            jax.ShapeDtypeStruct((count - split, rows, sum(cols)), jnp.bfloat16),
        ],
        name="sort_blocks",
    )(index, *grads)


class Chain:
    def __init__(self, steps):
        self.steps, self.result = steps, None
        self.flying = next(steps)

    def go(self, arrived):
        try:
            self.flying = self.steps.send(arrived)
        except StopIteration as end:
            self.flying, self.result = None, end.value


def boundary(values, *chains):
    live = [c for c in chains if c.flying is not None]
    values, arrived = lax.optimization_barrier((tuple(values), tuple(c.flying for c in live)))
    for chain, v in zip(live, arrived):
        chain.go(v)
    return values


def gather_steps(ring, own):
    rows = own.shape[0]
    back, ahead = [own], []
    back.append((yield ring.send(own)))
    for k in range(2, ring.steps + 1):
        v, w = yield ring.send(back[-1]), ring.core_swap(back[-1])
        back.append(v)
        ahead.append(w)
    last, w = yield ring.send(ring.half(back[-1], rows)), ring.core_swap(back[-1])
    ahead.append(w)
    other = yield ring.core_swap(last)
    return back + ahead + [last, other]


def reduce_index(ring):
    t, m = ring.table, ring.steps
    two = lambda v: (2 * v[:, None] + jnp.arange(2, dtype=jnp.int32)[None, :]).reshape(-1)
    opposite = 2 * ring.opposite.reshape(1)
    core = ring.core.reshape(1)
    return jnp.concatenate(
        [two(t[1 : m + 1]), opposite + 1 - core, two(t[m + 1 : 2 * m + 1]), opposite + core, two(t[:1])]
    )


def reduce_blocks(ring, grads):
    halves = [g.reshape(2 * ring.n, g.shape[0] // ring.n // 2, g.shape[1]) for g in grads]
    return sort_blocks(ring.index, 2 * ring.steps + 1, halves)


def reduce_steps(ring, outgoing, own):
    m, core = ring.steps, ring.core
    other = yield ring.core_swap(outgoing)
    got = yield ring.send(low(wide(own[2 * m : 2 * m + 1]) + wide(other[2 * m :])))
    for d in range(m, 0, -1):
        v = wide(own[2 * d - 2 : 2 * d]) + wide(other[2 * d - 2 : 2 * d])
        if d == m:
            at = lax.broadcasted_iota(jnp.int32, v.shape, 0)
            v = v + jnp.where(at == core, wide(got), 0.0)
        else:
            v = v + wide(got)
        got = yield ring.send(low(v))
    part = low(wide(own[2 * m + 1 :]) + wide(got))
    first = core == 0
    there = yield ring.core_swap(jnp.where(first, part[1], part[0]))
    both = low(wide(jnp.where(first, part[0], part[1])) + wide(there))
    there = yield ring.chip_swap(both)
    mine = low(wide(both) + wide(there))
    there = yield ring.core_swap(mine)
    out = jnp.stack([jnp.where(first, mine, there), jnp.where(first, there, mine)])
    return wide(out).reshape(2 * out.shape[1], out.shape[2])


def sum_steps(ring, v):
    v = v + (yield ring.core_swap(v))
    v = v + (yield ring.chip_swap(v))
    step = 1
    while step < ring.n:
        v = v + (yield lax.ppermute(v, "fsdp", [(i, i ^ step) for i in range(ring.n)]))
        step *= 2
    return v


def gelu_kernel(x_ref, w_ref, b_ref, act_ref, slope_ref):
    gelu_rows(x_ref, w_ref[...], b_ref[...], act_ref, slope_ref)


def gelu_rows(x_ref, w, b, act_ref, slope_ref):
    rows = 256
    for r in range(x_ref.shape[0] // rows):
        at = slice(r * rows, (r + 1) * rows)
        h = jnp.dot(x_ref[at, :], w, preferred_element_type=jnp.float32) + b
        size = jnp.abs(h)
        t = 1.0 / (1.0 + (0.3275911 * 0.7071067811865476) * size)
        e = jnp.exp(-0.5 * h * h)
        poly = t * (
            0.5 * 0.254829592
            + t * (-0.5 * 0.284496736 + t * (0.5 * 1.421413741 + t * (-0.5 * 1.453152027 + t * (0.5 * 1.061405429))))
        )
        tail = poly * e
        upper = jnp.where(h >= 0.0, 1.0 - tail, tail)
        act_ref[at, :] = (h * upper).astype(jnp.bfloat16)
        slope_ref[at, :] = (upper + (h * 0.3989422804014327) * e).astype(jnp.bfloat16)


TILE = 512


def gelu_layer(x, w, b):
    rows, width = x.shape
    ff = w.shape[1]
    out = pl.BlockSpec((rows, TILE), lambda j: (0, j))
    return pl.pallas_call(
        gelu_kernel,
        grid=(ff // TILE,),
        in_specs=[
            pl.BlockSpec((rows, width), lambda j: (0, 0)),
            pl.BlockSpec((width, TILE), lambda j: (0, j)),
            pl.BlockSpec((1, TILE), lambda j: (0, j)),
        ],
        out_specs=[out, out],
        out_shape=[jax.ShapeDtypeStruct((rows, ff), jnp.bfloat16)] * 2,
        name="gelu_layer",
    )(x, w, b)


def gelu_ring(x, table, pieces, b, n, part, before=()):
    rows, width = x.shape
    shard, ff = pieces[0].shape
    half = shard // 2
    steps = ff // TILE // PARTS
    off = part * steps

    def kernel(table_ref, x_ref, b_ref, *refs):
        ins = refs[: len(pieces)]
        act_ref, slope_ref, w_ref = refs[-3:]

        def write(f, h, ref, first):
            w_ref[f, h] = ref[first * half : (first + 1) * half, :]

        place_pieces(table_ref, ins, write)
        gelu_rows(x_ref, w_ref[...].reshape(width, TILE), b_ref[...], act_ref, slope_ref)

    out = pl.BlockSpec((rows, TILE), lambda j, t: (0, off + j))
    first = 3 + len(pieces)
    act, slope, w = pl.pallas_call(
        kernel,
        grid_spec=pltpu.PrefetchScalarGridSpec(
            num_scalar_prefetch=1,
            grid=(steps,),
            in_specs=[
                pl.BlockSpec((rows, width), lambda j, t: (0, 0)),
                pl.BlockSpec((1, TILE), lambda j, t: (0, off + j)),
            ]
            + [pl.BlockSpec((p.shape[0], TILE), lambda j, t: (0, off + j)) for p in pieces]
            + [ANY] * len(before),
            out_specs=[out, out, pl.BlockSpec((n, 2, half, TILE), lambda j, t: (0, 0, 0, off + j))],
        ),
        out_shape=[jax.ShapeDtypeStruct((rows, ff), jnp.bfloat16)] * 2
        + [jax.ShapeDtypeStruct((n, 2, half, ff), jnp.bfloat16)],
        input_output_aliases={first + i: i for i in range(len(before))},
        name=f"gelu_ring_{part}",
    )(table, x, b, *pieces, *before)
    return act, slope, w


def hidden_back(d_branch, slope, table, pieces, n):
    rows, width = d_branch.shape
    shard = pieces[0].shape[0]
    half = shard // 2

    def kernel(table_ref, d_ref, slope_ref, *refs):
        ins = refs[: len(pieces)]
        out_ref, sum_ref, w_ref = refs[-3:]
        k = pl.program_id(0)
        core = table_ref[n]
        for j in range(n - 1):

            @pl.when(k == j)
            def _(j=j):
                w_ref[0, 0] = ins[j][:half]
                w_ref[0, 1] = ins[j][half:]

        @pl.when(k == n - 1)
        def _():
            w_ref[0, core] = ins[n - 1][...]
            w_ref[0, 1 - core] = ins[n][...]

        w = w_ref[...].reshape(shard, width)
        total = jnp.zeros((1, shard), jnp.float32)
        for r in range(rows // 256):
            at = slice(r * 256, (r + 1) * 256)
            v = dotf(d_ref[at, :], w, 1, 1) * slope_ref[at, :].astype(jnp.float32)
            v = v.astype(jnp.bfloat16)
            out_ref[at, :] = v
            total += jnp.sum(v.astype(jnp.float32), axis=0, keepdims=True)
        sum_ref[...] = total

    vm = lambda: pl.BlockSpec(memory_space=pltpu.VMEM)
    block = pl.BlockSpec((rows, shard), lambda k, t: (0, t[k]))
    out, total, w = pl.pallas_call(
        kernel,
        grid_spec=pltpu.PrefetchScalarGridSpec(
            num_scalar_prefetch=1,
            grid=(n,),
            in_specs=[pl.BlockSpec((rows, width), lambda k, t: (0, 0)), block] + [vm() for _ in pieces],
            out_specs=[
                block,
                pl.BlockSpec((1, shard), lambda k, t: (0, t[k])),
                pl.BlockSpec((1, 2, half, width), lambda k, t: (t[k], 0, 0, 0)),
            ],
        ),
        out_shape=[
            jax.ShapeDtypeStruct((rows, n * shard), jnp.bfloat16),
            jax.ShapeDtypeStruct((1, n * shard), jnp.float32),
            jax.ShapeDtypeStruct((n, 2, half, width), jnp.bfloat16),
        ],
        name="hidden_back",
    )(table, d_branch, slope, *pieces)
    return out, total, w.reshape(n * shard, width)


def norm_parts(v):
    c = v - jnp.mean(v, axis=-1, keepdims=True)
    r = lax.rsqrt(jnp.mean(c * c, axis=-1, keepdims=True) + epsilon)
    return c * r, r


def column_sum(v):
    return jnp.sum(v.astype(jnp.float32), axis=0)


def norm_back(dn, x, r, gain):
    u = dn * gain
    e = r * (u - jnp.mean(u, axis=-1, keepdims=True) - x * jnp.mean(u * x, axis=-1, keepdims=True))
    return e, column_sum(dn * x), column_sum(dn)


def matmul(a, b, ca, cb):
    return lax.dot_general(a, b, (((ca,), (cb,)), ((), ())), preferred_element_type=jnp.float32)


def pair_order(v, width):
    return v.reshape(v.shape[0], 3, width // PAIR, PAIR).transpose(0, 2, 1, 3).reshape(v.shape[0], 3 * width)


def natural_order(vs, width):
    pick = lambda h, g: vs[h // GROUP][:, (h % GROUP * 3 + g) * PAIR : (h % GROUP * 3 + g + 1) * PAIR]
    return jnp.concatenate([pick(h, g) for g in range(3) for h in range(width // PAIR)], axis=1)


def halves(v):
    return [v[:, j * 3 * GROUP * PAIR : (j + 1) * 3 * GROUP * PAIR] for j in range(PARTS)]


def qkv_shift(vec):
    rows = [vec[2:3], jnp.zeros_like(vec[2:3]), vec[3:4]]
    return pair_order(jnp.concatenate(rows, axis=1), vec.shape[1])


def pack_small(rows, b1, n):
    shard = rows.shape[1] // n

    def kernel(rows_ref, b1_ref, out_ref):
        out_ref[...] = jnp.zeros_like(out_ref)
        every, line = rows_ref[...], b1_ref[...]
        for f in range(n):
            out_ref[f, 0:8, 0:shard] = every[:, f * shard : (f + 1) * shard]
            for r in range(4):
                first = (4 * f + r) * shard
                out_ref[f, 8 + r : 9 + r, 0:shard] = line[:, first : first + shard]

    return pl.pallas_call(
        kernel, out_shape=jax.ShapeDtypeStruct((n, 16, PAIR), jnp.float32), name="pack_small"
    )(rows, b1)


def layer_ring(n, dp, tokens, segment_ids, cotangent, params):
    (ln1_gain, ln1_bias, qkv_weight, query_bias, value_bias, proj_weight, proj_bias) = params[:7]
    (ln2_gain, ln2_bias, fc1_weight, fc1_bias, fc2_weight, fc2_bias) = params[7:]
    _, seq, width = tokens.shape
    shard = ln1_gain.shape[0]
    ff = fc1_weight.shape[1]
    ring = Ring(n, dp)
    table = ring.table
    swap = ring.core_swap

    eight = jnp.stack([ln1_gain, ln1_bias, query_bias, value_bias, proj_bias, ln2_gain, ln2_bias, fc2_bias])
    four = fc1_bias.reshape(4, shard)
    small = jnp.concatenate(
        [jnp.pad(eight, ((0, 0), (0, PAIR - shard))), jnp.pad(four, ((0, 4), (0, 4 * width - PAIR - shard)))], axis=1
    )
    top = jnp.concatenate([jnp.concatenate([qkv_weight, proj_weight], axis=1), small], axis=0)
    a = [top]
    for _ in range(ring.steps):
        a.append(ring.send(a[-1]))
    a_last = ring.send(jnp.concatenate([ring.half(a[-1][:shard], shard), a[-1][shard:]], axis=0))
    pieces = a + [swap(v) for v in a[1:]] + [a_last, swap(a_last)]
    wqkv, wproj, vec, b_fc1 = assemble_first(table, pieces, n, shard, width, shard)
    g1, b1, bp, g2, b2, b_fc2 = (vec[j : j + 1] for j in (0, 1, 4, 5, 6, 7))

    c0, _ = tie(fc1_weight, a_last)
    g_fc1 = Chain(gather_steps(ring, c0))
    flat = wide(tokens.reshape(seq, width))
    seg = segment_ids.reshape(seq)
    x1, r1 = norm_parts(flat)
    n1 = low(x1 * g1 + b1)
    qkv = low(matmul(n1, wqkv, 1, 0) + qkv_shift(vec))
    (qkv,) = boundary([qkv], g_fc1)
    ctx, lse = boundary(attention(qkv, seg, 0), g_fc1)
    ctx, lse = boundary(attention(qkv, seg, 1, (ctx, lse)), g_fc1)
    middle = wide(tokens.reshape(seq, width)) + (matmul(ctx, wproj, 1, 0) + bp)
    x2, r2 = norm_parts(middle)
    n2 = low(x2 * g2 + b2)
    (n2,) = boundary([n2], g_fc1)
    e0, _ = tie(fc2_weight, g_fc1.flying)
    g_fc2 = Chain(gather_steps(ring, e0))
    g_fc1.go(g_fc1.flying)
    before = boundary(gelu_ring(n2, table, g_fc1.result, b_fc1, n, 0), g_fc2)
    act, slope, w1 = gelu_ring(n2, table, g_fc1.result, b_fc1, n, 1, before)
    w1 = w1.reshape(width, ff)
    d_branch = cotangent.reshape(seq, width)
    (act,) = boundary([act], g_fc2)
    (grad_fc2,) = boundary([low(matmul(act, d_branch, 0, 0))], g_fc2)
    blocks = boundary(reduce_blocks(ring, [grad_fc2]), g_fc2)
    r_fc2 = Chain(reduce_steps(ring, *blocks))
    g_fc2.go(g_fc2.flying)
    d_hidden, grad_fc1_bias, w2 = hidden_back(d_branch, slope, table, g_fc2.result, n)
    (d_hidden,) = boundary([d_hidden], r_fc2)
    (grad_fc1,) = boundary([low(matmul(n2, d_hidden, 0, 0))], r_fc2)
    r_fc1 = Chain(reduce_steps(ring, *reduce_blocks(ring, [grad_fc1])))
    d_norm_two = matmul(d_hidden, w1, 1, 1)
    e2, grad_ln2_gain, grad_ln2_bias = norm_back(d_norm_two, x2, r2, g2)
    d_middle = wide(d_branch) + e2
    d_attn = low(d_middle)
    (d_attn,) = boundary([d_attn], r_fc2, r_fc1)
    grad_proj = low(matmul(ctx, d_attn, 0, 0))
    d_ctx = low(matmul(d_attn, wproj, 1, 1))
    d_ctx, grad_proj = boundary([d_ctx, grad_proj], r_fc2, r_fc1)
    d_qkv, sums = boundary(attention_back(qkv, seg, d_ctx, lse, 0), r_fc2, r_fc1)
    cut = 3 * GROUP * PAIR
    blocks = reduce_blocks(ring, [low(matmul(n1, d_qkv[:, :cut], 0, 0)), grad_proj])
    *blocks, d_qkv, sums = boundary([*blocks, d_qkv, sums], r_fc2, r_fc1)
    r_one = Chain(reduce_steps(ring, *blocks))
    d_qkv, sums = boundary(attention_back(qkv, seg, d_ctx, lse, 1, (d_qkv, sums)), r_fc2, r_fc1, r_one)
    blocks = reduce_blocks(ring, [low(matmul(n1, d_qkv[:, cut:], 0, 0))])
    *blocks, d_qkv = boundary([*blocks, d_qkv], r_fc2, r_fc1, r_one)
    r_two = Chain(reduce_steps(ring, *blocks))
    chains = [r_fc2, r_fc1, r_one, r_two]
    (d_norm_one,) = boundary([matmul(d_qkv, wqkv, 1, 1)], *chains)
    e1, grad_ln1_gain, grad_ln1_bias = norm_back(d_norm_one, x1, r1, g1)
    input_grad = d_middle + e1
    sums = natural_order(halves(sums), width).reshape(-1)
    rows = [
        grad_ln1_gain,
        grad_ln1_bias,
        sums[:width],
        sums[2 * width :],
        column_sum(d_attn),
        grad_ln2_gain,
        grad_ln2_bias,
        column_sum(d_branch),
    ]
    tiny = pack_small(jnp.stack(rows), grad_fc1_bias, n)
    tiny, input_grad, act = boundary([tiny, input_grad, act], *chains)
    chains.append(Chain(sum_steps(ring, tiny)))
    layer_out = low(middle + (matmul(act, w2, 1, 0) + b_fc2))
    (layer_out,) = boundary([layer_out], *chains)
    while any(c.flying is not None for c in chains):
        boundary([], *chains)
    mine = lax.dynamic_index_in_dim(chains[-1].result, table[0], 0, keepdims=False)
    line = [mine[j, :shard] for j in range(8)]
    out_qkv = natural_order([r_one.result[:, :cut], r_two.result], width)
    return (
        layer_out.reshape(tokens.shape),
        input_grad.reshape(tokens.shape),
        line[0],
        line[1],
        out_qkv,
        line[2],
        line[3],
        r_one.result[:, cut:],
        line[4],
        line[5],
        line[6],
        r_fc1.result,
        mine[8:12, :shard].reshape(4 * shard),
        r_fc2.result,
        line[7],
    )


def layer_plain(tokens, segment_ids, cotangent, params):
    gather = lambda v: lax.all_gather(v, "fsdp", axis=0, tiled=True)
    whole = [gather(v) for v in params]
    vec = wide(jnp.stack([whole[j] for j in (0, 1, 3, 4, 6, 7, 8, 12)]))
    _, seq, width = tokens.shape
    wqkv, wproj, w1, w2 = pair_order(whole[2], width), whole[5], whole[9], whole[11]
    b_fc1 = wide(whole[10]).reshape(1, -1)
    g1, b1, bp, g2, b2, b_fc2 = (vec[j : j + 1] for j in (0, 1, 4, 5, 6, 7))
    flat = wide(tokens.reshape(seq, width))
    seg = segment_ids.reshape(seq)
    x1, r1 = norm_parts(flat)
    n1 = low(x1 * g1 + b1)
    qkv = low(matmul(n1, wqkv, 1, 0) + qkv_shift(vec))
    kept = attention(qkv, seg, 0)
    ctx, lse = attention(qkv, seg, 1, kept)
    middle = flat + (matmul(ctx, wproj, 1, 0) + bp)
    x2, r2 = norm_parts(middle)
    n2 = low(x2 * g2 + b2)
    act, slope = gelu_layer(n2, w1, b_fc1)
    layer_out = low(middle + (matmul(act, w2, 1, 0) + b_fc2))
    d_branch = cotangent.reshape(seq, width)
    d_hidden = low(matmul(d_branch, w2, 1, 1) * wide(slope))
    e2, grad_ln2_gain, grad_ln2_bias = norm_back(matmul(d_hidden, w1, 1, 1), x2, r2, g2)
    d_middle = wide(d_branch) + e2
    d_attn = low(d_middle)
    d_ctx = low(matmul(d_attn, wproj, 1, 1))
    kept = attention_back(qkv, seg, d_ctx, lse, 0)
    d_qkv, sums = attention_back(qkv, seg, d_ctx, lse, 1, kept)
    sums = natural_order(halves(sums), width)
    e1, grad_ln1_gain, grad_ln1_bias = norm_back(matmul(d_qkv, wqkv, 1, 1), x1, r1, g1)

    def reduce(v):
        return lax.psum(lax.psum_scatter(v, "fsdp", scatter_dimension=0, tiled=True), "dp")

    line = lambda v: reduce(v.reshape(-1))
    return (
        layer_out.reshape(tokens.shape),
        (d_middle + e1).reshape(tokens.shape),
        line(grad_ln1_gain),
        line(grad_ln1_bias),
        natural_order(halves(reduce(matmul(n1, d_qkv, 0, 0))), width),
        line(sums[:, :width]),
        line(sums[:, 2 * width :]),
        reduce(matmul(ctx, d_attn, 0, 0)),
        line(column_sum(d_attn)),
        line(grad_ln2_gain),
        line(grad_ln2_bias),
        reduce(matmul(n2, d_hidden, 0, 0)),
        line(column_sum(d_hidden)),
        reduce(matmul(act, d_branch, 0, 0)),
        line(column_sum(d_branch)),
    )


def per_device(n, dp, tokens, segment_ids, cotangent, *params):
    small_ring = dp == 4 and 4 <= n <= RING_MAX and n & (n - 1) == 0
    if small_ring and params[0].shape[0] % 16 == 0:
        return layer_ring(n, dp, tokens, segment_ids, cotangent, params)
    return layer_plain(tokens, segment_ids, cotangent, params)


def solution(mesh):
    n, dp = mesh.shape["fsdp"], mesh.shape["dp"]
    rows = P(("fsdp", "dp"), None, None)
    vec, mat = P("fsdp"), P("fsdp", None)
    params = (vec, vec, mat, vec, vec, mat, vec, vec, vec, mat, vec, mat, vec)
    return jax.shard_map(
        lambda *args: per_device(n, dp, *args),
        mesh=mesh,
        in_specs=(rows, P(("fsdp", "dp"), None), rows) + params,
        out_specs=(rows, rows) + params,
        check_vma=False,
    )
```
